512 devices in a mesh: req: 64 (over y, z), tp: 8 (over x, core).
Axes of the slice: x: 4, y: 4, z: 16, core: 2. Of those that a mesh axis runs over, the one named last changes fastest.
Arguments:
- hidden_in: bfloat16 [4, 256, 3072], P(None, 'req', 'tp'), may hold values from -6 to 6
- norm_gain: float32 [3072], replicated, may hold values from 0.1 to 1.9
- w_query: bfloat16 [3072, 2048], P(None, 'tp'), may hold values from -1 to 1
- w_key: bfloat16 [3072, 1024], P(None, 'tp'), may hold values from -1 to 1
- w_value: bfloat16 [3072, 1024], P(None, 'tp'), may hold values from -0.109375 to 0.109375
- w_out: bfloat16 [2048, 3072], P('tp'), may hold values from -0.125 to 0.125
- prompt_keys: bfloat16 [64, 512, 1024], P('req', None, 'tp'), may hold values from -100 to 100
- prompt_values: bfloat16 [64, 512, 1024], P('req', None, 'tp'), may hold values from -8 to 8
- gen_keys: bfloat16 [256, 64, 1024], P('req', None, 'tp'), may hold values from -9 to 9
- gen_values: bfloat16 [256, 64, 1024], P('req', None, 'tp'), may hold values from -8 to 8
- lengths: int32 [32], replicated, may hold values from 768 to 1024, as said below
- parents: int32 [4, 256], replicated, may hold values from 0 to 7
Outputs:
- attended: bfloat16 [4, 256, 3072], P(None, 'req', 'tp')
The draws below stay inside these ranges and needn't reach their ends.
Inputs may be any that keep to these rules, and one draw needn't show every extreme that they name: `lengths`: one request has a prompt of exactly 1024 tokens.
All inputs are finite; a program needn't handle non-finite values.
Results may differ from the reference program's by a relative error of at most 0.028.
Values may be sent and summed in bfloat16 or wider, within the bound.
A program may use at most 64 MiB of HBM per device.

```python
import jax
import jax.numpy as jnp
from jax import lax

D = 3072
KVH = 8
HD = 128
QH = 16
BEAMS = 8
STEPS = 4
PROMPT_MAX = 1024
GEN0 = 64
REQUESTS = 32
HALF = 512


def draw_lengths(key, part):
    drawn = jax.random.randint(key, (REQUESTS,), 3 * PROMPT_MAX // 4, PROMPT_MAX + 1, dtype=jnp.int32)
    longest = jax.random.randint(jax.random.fold_in(key, 7), (), 0, REQUESTS, dtype=jnp.int32)
    return jnp.where(jnp.arange(REQUESTS, dtype=jnp.int32) == longest, PROMPT_MAX, drawn).astype(jnp.int32)


def shared_query(key):
    return jax.random.truncated_normal(jax.random.fold_in(key, 11), -4.0, 4.0, (D, QH * HD), jnp.float32) * D ** (-0.5)


def draw_w_query(key, part):
    return shared_query(key).astype(jnp.bfloat16)


def draw_w_key(key, part):
    q_group = QH // KVH
    query_heads = shared_query(key).reshape(D, KVH, q_group, HD)
    picked = jax.random.randint(jax.random.fold_in(key, 13), (KVH,), 0, q_group, dtype=jnp.int32)
    chosen = jnp.take_along_axis(query_heads, picked[None, :, None, None], axis=2)[:, :, 0, :]
    mixing = jax.random.uniform(jax.random.fold_in(key, 17), (KVH,), jnp.float32, 0.35, 0.75)
    rest = jnp.sqrt(1.0 - mixing * mixing)
    noise = jax.random.truncated_normal(jax.random.fold_in(key, 19), -4.0, 4.0, (D, KVH, HD), jnp.float32) * D ** (-0.5)
    mixed = mixing[None, :, None] * chosen + rest[None, :, None] * noise
    return mixed.reshape(D, KVH * HD).astype(jnp.bfloat16)


def draw_prompt_keys(key, part):
    shape = (REQUESTS * 2, HALF, KVH * HD)
    base = 1.5 * jax.random.truncated_normal(key, -6.0, 6.0, shape, jnp.float32)
    return base.astype(jnp.bfloat16)


def set_ends(entries, stream_key, least, high):
    extent = entries.shape
    index_at = [jax.random.randint(jax.random.fold_in(stream_key, axis), (), 0, extent[axis]) for axis in range(len(extent))]
    entries = entries.at[tuple(index_at)].set(least)
    longest = extent.index(max(extent))
    index_at[longest] = (index_at[longest] + 1) % extent[longest]
    return entries.at[tuple(index_at)].set(high)


def block_levels(rng, shape, pieces, low, top_value):
    level = 1.0
    for position, parts in pieces:
        heights = jax.random.uniform(jax.random.fold_in(jax.random.fold_in(rng, 6), position), (parts,), jnp.float32, low / len(pieces), top_value / len(pieces))
        level = level * jnp.repeat(jnp.exp(heights), shape[position] // parts).reshape((-1,) + (1,) * (len(shape) - 1 - position))
    return level


def bell_draw(rng, extent, scale, limit, pieces=(), kind=jnp.bfloat16):
    result = scale * jax.random.normal(rng, extent, jnp.float32)
    if pieces:
        result = result * block_levels(rng, extent, pieces, -0.22, 0.18)
    return jnp.clip(result, -limit, limit).astype(kind)


def setup_inputs(seed: int = 0) -> dict:
    key_list = jax.random.split(jax.random.key(seed), 13)
    hidden_in = bell_draw(key_list[0], (STEPS, REQUESTS * BEAMS, D), 1.0, 6.0, ((1, 64), (2, 8)))
    norm_gain = jnp.clip(1.0 + 0.18 * jax.random.normal(key_list[1], (D,), jnp.float32), 0.1, 1.9)
    w_query = draw_w_query(jax.random.fold_in(key_list[12], 71), 0)
    w_key = draw_w_key(jax.random.fold_in(key_list[12], 71), 0)
    w_value = bell_draw(key_list[4], (D, KVH * HD), D ** -0.5, 0.109375, ((1, 8),))
    w_out = bell_draw(key_list[5], (QH * HD, D), (QH * HD) ** -0.5, 0.125, ((0, 8),))
    prompt_keys = draw_prompt_keys(jax.random.fold_in(key_list[12], 71), 0)
    prompt_values = bell_draw(key_list[7], (REQUESTS * 2, HALF, KVH * HD), 2.0, 8.0, ((0, 64), (2, 8)))
    gen_keys = bell_draw(key_list[8], (REQUESTS * BEAMS, GEN0, KVH * HD), 1.5, 9.0, ((0, 64), (2, 8)))
    gen_values = bell_draw(key_list[9], (REQUESTS * BEAMS, GEN0, KVH * HD), 2.0, 8.0, ((0, 64), (2, 8)))
    lengths = draw_lengths(jax.random.fold_in(key_list[12], 71), 0)
    parents = set_ends(jax.random.randint(key_list[11], (STEPS, REQUESTS * BEAMS), 0, BEAMS), jax.random.fold_in(key_list[11], 1), 0, BEAMS - 1).astype(jnp.int32)
    return dict(hidden_in=hidden_in, norm_gain=norm_gain, w_query=w_query, w_key=w_key, w_value=w_value, w_out=w_out, prompt_keys=prompt_keys, prompt_values=prompt_values, gen_keys=gen_keys, gen_values=gen_values, lengths=lengths, parents=parents)


norm_eps = 1e-05
masked_score = -1e+30
rope_base = 500000.0

def rotate(vectors, positions):
    half_dim = vectors.shape[-1] // 2
    inverse = rope_base ** (-jnp.arange(half_dim, dtype=jnp.float32) / half_dim)
    angles = positions.astype(jnp.float32)[:, None, None] * inverse
    cosine = jnp.cos(angles)
    sine_part = jnp.sin(angles)
    first = vectors[..., :half_dim]
    second = vectors[..., half_dim:]
    return jnp.concatenate([first * cosine - second * sine_part, second * cosine + first * sine_part], axis=-1)

def reference(hidden_in, norm_gain, w_query, w_key, w_value, w_out, prompt_keys, prompt_values, gen_keys, gen_values, lengths, parents):
    beam_rows = hidden_in.shape[1]
    requests = beam_rows // BEAMS
    q_group = QH // KVH
    scaling = HD ** (-0.5)
    prompt_k = prompt_keys.reshape(requests, 2 * HALF, KVH, HD).astype(jnp.float32)
    prompt_v = prompt_values.reshape(requests, 2 * HALF, KVH, HD).astype(jnp.float32)
    cache_k = gen_keys.reshape(requests, BEAMS, GEN0, KVH, HD)
    cache_v = gen_values.reshape(requests, BEAMS, GEN0, KVH, HD)
    usable = jnp.arange(2 * HALF, dtype=jnp.int32)[None, :] < lengths[:, None]
    choose = jax.vmap(lambda table, index: table[index])
    results = []
    for step in range(STEPS):
        inputs = hidden_in[step].astype(jnp.float32)
        inverse = lax.rsqrt(lax.optimization_barrier(jnp.mean(inputs * inputs, axis=-1, keepdims=True)) + norm_eps)
        normed = (inputs * inverse * norm_gain).astype(jnp.bfloat16)
        positions = jnp.repeat(lengths + GEN0 + step, BEAMS).astype(jnp.int32)
        queries = jnp.dot(normed, w_query, preferred_element_type=jnp.float32).reshape(beam_rows, QH, HD)
        queries = rotate(queries, positions).astype(jnp.bfloat16).reshape(requests, BEAMS, KVH, q_group, HD)
        new_k = jnp.dot(normed, w_key, preferred_element_type=jnp.float32).reshape(beam_rows, KVH, HD)
        new_k = rotate(new_k, positions).astype(jnp.bfloat16).reshape(requests, BEAMS, KVH, HD)
        new_v = jnp.dot(normed, w_value, preferred_element_type=jnp.float32).astype(jnp.bfloat16).reshape(requests, BEAMS, KVH, HD)
        chosen = parents[step].reshape(requests, BEAMS)
        cache_k = jnp.concatenate([choose(cache_k, chosen), new_k[:, :, None]], axis=2)
        cache_v = jnp.concatenate([choose(cache_v, chosen), new_v[:, :, None]], axis=2)
        query_f = queries.astype(jnp.float32)
        prompt_scores = jnp.einsum('rbkgd,rpkd->rbkgp', query_f, prompt_k) * scaling
        prompt_scores = jnp.where(usable[:, None, None, None, :], prompt_scores, masked_score)
        cache_scores = jnp.einsum('rbkgd,rbtkd->rbkgt', query_f, cache_k.astype(jnp.float32)) * scaling
        weights = jax.nn.softmax(jnp.concatenate([prompt_scores, cache_scores], axis=-1), axis=-1)
        weights = lax.optimization_barrier(weights.astype(jnp.bfloat16)).astype(jnp.float32)
        context = jnp.einsum('rbkgp,rpkd->rbkgd', weights[..., :2 * HALF], prompt_v)
        context = context + jnp.einsum('rbkgt,rbtkd->rbkgd', weights[..., 2 * HALF:], cache_v.astype(jnp.float32))
        context = context.astype(jnp.bfloat16).reshape(beam_rows, QH * HD)
        results.append(jnp.dot(context, w_out, preferred_element_type=jnp.float32).astype(jnp.bfloat16))
    return jnp.stack(results)
```

```python
import math

import jax
import jax.numpy as jnp
from jax import lax
from jax.experimental import pallas as pl
from jax.experimental.pallas import tpu as pltpu
from jax.sharding import PartitionSpec as P

HD = 128
TP = 8
STEPS = 4
OWN = 4
BEAMS = 8
ROWS = STEPS * OWN
BLK = 384
D = TP * BLK
HALF = 512
GEN = 64
KEYS = HALF + OWN * GEN + 128
NEW = HALF + OWN * GEN
EPS = 1e-05
NEG = -1e30
ROPE_BASE = 500000.0
NEAR = (1, 2, 3, 6, 7, 4, 5)
FAR = (4, 5, 2, 3, 6, 7, 1)

bf16 = jnp.bfloat16
f32 = jnp.float32


def flip(index, k):
    result = 0
    for bit in (1, 2, 4):
        digit = (index // bit) % 2
        result += bit * ((1 - digit) if k & bit else digit)
    return result


def attend(q, kk, vv, bias):
    s = lax.dot_general(q, kk[...], (((1,), (1,)), ((), ())), preferred_element_type=f32)
    s = s * (HD**-0.5) + bias
    m = jnp.max(s, axis=-1, keepdims=True)
    p = jnp.exp(s - m)
    l = jnp.sum(p, axis=-1, keepdims=True)
    o = jnp.dot(p.astype(bf16), vv[...], preferred_element_type=f32)
    return m, l, o


def kernel(
    hidden, gain, wq, wk, wv, wo, pk, pv, gk, gv, lengths, parents,
    out,
    xin, xsend, xbuf, gainv, wqv, wkv, wvv, wov, kk, vv, lens, par, bias,
    qsend, qrecv, psend, precv, osend, orecv,
    in_sem, wq_sem, wk_sem, wv_sem, wo_sem, gk_sem, gv_sem,
    xs_sem, xr_sem, q_sem, p_sem, os_sem, or_sem,
):
    req = lax.axis_index("req")
    tp = lax.axis_index("tp")
    parity = req % 2
    request = req // 2
    partner = req + 1 - 2 * parity
    peer = [flip(tp, k) for k in range(TP)]

    local = [
        pltpu.make_async_copy(hidden, xin, in_sem.at[0]),
        pltpu.make_async_copy(gain, gainv, in_sem.at[1]),
        pltpu.make_async_copy(lengths, lens, in_sem.at[2]),
        pltpu.make_async_copy(parents, par, in_sem.at[3]),
        pltpu.make_async_copy(pk, kk.at[pl.ds(0, HALF)], in_sem.at[4]),
        pltpu.make_async_copy(pv, vv.at[pl.ds(0, HALF)], in_sem.at[5]),
    ]
    local[0].start()

    barrier = pltpu.get_barrier_semaphore()
    for k in range(1, TP):
        pl.semaphore_signal(
            barrier, inc=1, device_id={"tp": peer[k]}, device_id_type=pl.DeviceIdType.MESH
        )
    pl.semaphore_signal(
        barrier, inc=1, device_id={"req": partner}, device_id_type=pl.DeviceIdType.MESH
    )

    for copy in local[1:4]:
        copy.start()
    weights = []
    for k in (0,) + NEAR:
        rows = pl.ds(pl.multiple_of(peer[k] * BLK, BLK), BLK)
        mine = [
            pltpu.make_async_copy(wq.at[rows], wqv.at[k], wq_sem.at[k]),
            pltpu.make_async_copy(wk.at[rows], wkv.at[k], wk_sem.at[k]),
            pltpu.make_async_copy(wv.at[rows], wvv.at[k], wv_sem.at[k]),
        ]
        for copy in mine:
            copy.start()
        weights.append(mine)

    local[0].wait()
    x = xin[...].astype(f32)
    x = jnp.concatenate([x[s] for s in range(STEPS)], axis=0)
    xsend[...] = x.astype(bf16)
    pl.semaphore_wait(barrier, TP)
    xcopy = {}
    for k in FAR:
        xcopy[k] = pltpu.make_async_remote_copy(
            src_ref=xsend,
            dst_ref=xbuf.at[k],
            send_sem=xs_sem.at[k],
            recv_sem=xr_sem.at[k],
            device_id={"tp": peer[k]},
            device_id_type=pl.DeviceIdType.MESH,
        )
        xcopy[k].start()

    local[4].start()
    local[5].start()
    caches = []
    for b in range(OWN):
        there = pl.ds(HALF + b * GEN, GEN)
        caches.append(pltpu.make_async_copy(gk.at[b], kk.at[there], gk_sem.at[b]))
        caches.append(pltpu.make_async_copy(gv.at[b], vv.at[there], gv_sem.at[b]))
    for copy in caches:
        copy.start()
    outw = {}
    for k in FAR + (0,):
        cols = pl.ds(pl.multiple_of(peer[k] * BLK, BLK), BLK)
        outw[k] = pltpu.make_async_copy(wo.at[:, cols], wov.at[k], wo_sem.at[k])
        outw[k].start()

    local[2].wait()
    local[3].wait()
    length = lens[request]
    row = lax.broadcasted_iota(jnp.int32, (ROWS, HD), 0)
    lane = lax.broadcasted_iota(jnp.int32, (ROWS, HD), 1)
    position = (length + GEN + row // OWN).astype(f32)
    frequency = jnp.exp((lane % (HD // 2)).astype(f32) * (-math.log(ROPE_BASE) / (HD // 2)))
    angle = position * frequency
    cosine = jnp.cos(angle)
    sine = jnp.sin(angle)
    sine = jnp.where(lane < HD // 2, -sine, sine)

    wide = lax.broadcasted_iota(jnp.int32, (ROWS, HALF), 1)
    prompt_bias = jnp.where(parity * HALF + wide < length, 0.0, NEG).astype(f32)
    gen_beam = OWN * parity + lax.broadcasted_iota(jnp.int32, (ROWS, OWN * GEN), 1) // GEN
    zero = jnp.zeros((128, HD), bf16)
    kk[pl.ds(NEW, 128), :] = zero
    vv[pl.ds(NEW, 128), :] = zero
    for side in range(2):
        first = OWN * (parity if side == 0 else 1 - parity)
        gen_from = jnp.zeros((ROWS, HD), jnp.int32)
        new_from = jnp.full((ROWS, HD), -1, jnp.int32)
        for s in range(STEPS):
            for b in range(OWN):
                here = row == s * OWN + b
                at = first + b
                for t in range(s, -1, -1):
                    new_from = jnp.where(here & (lane // OWN == t), at, new_from)
                    at = par[t, request * BEAMS + at]
                gen_from = jnp.where(here, at, gen_from)
        gen_from = jnp.concatenate([gen_from, gen_from], axis=1)
        gen_bias = jnp.where(gen_from == gen_beam, 0.0, NEG).astype(f32)
        new_bias = jnp.where(new_from == OWN * parity + lane % OWN, 0.0, NEG).astype(f32)
        table = jnp.concatenate([prompt_bias, gen_bias, new_bias], axis=1)
        bias[side, pl.ds(0, ROWS), :] = table
        bias[side, pl.ds(ROWS, ROWS), :] = table

    local[1].wait()
    acc_q = jnp.zeros((ROWS, 2 * HD), f32)
    acc_k = jnp.zeros((ROWS, HD), f32)
    acc_v = jnp.zeros((ROWS, HD), f32)
    squares = jnp.zeros((ROWS, HD), f32)
    for i, k in enumerate((0,) + NEAR):
        if k:
            xcopy[k].wait_recv()
            x = xbuf[k].astype(f32)
        for copy in weights[i]:
            copy.wait()
        for c in range(BLK // HD):
            part = x[:, c * HD : (c + 1) * HD]
            squares = squares + part * part
        scaled = (x * gainv[peer[k]]).astype(bf16)
        acc_q = acc_q + jnp.dot(scaled, wqv[k], preferred_element_type=f32)
        acc_k = acc_k + jnp.dot(scaled, wkv[k], preferred_element_type=f32)
        acc_v = acc_v + jnp.dot(scaled, wvv[k], preferred_element_type=f32)
    inverse = lax.rsqrt(jnp.sum(squares, axis=-1, keepdims=True) / D + EPS)

    def rotated(value):
        value = value * inverse
        return (value * cosine + pltpu.roll(value, HD // 2, 1) * sine).astype(bf16)

    own_q = jnp.concatenate([rotated(acc_q[:, :HD]), rotated(acc_q[:, HD:])], axis=0)
    qsend[...] = own_q
    qcopy = pltpu.make_async_remote_copy(
        src_ref=qsend,
        dst_ref=qrecv,
        send_sem=q_sem.at[0],
        recv_sem=q_sem.at[1],
        device_id={"req": partner},
        device_id_type=pl.DeviceIdType.MESH,
    )
    qcopy.start()
    kk[pl.ds(NEW, ROWS), :] = rotated(acc_k)
    vv[pl.ds(NEW, ROWS), :] = (acc_v * inverse).astype(bf16)

    local[4].wait()
    local[5].wait()
    for copy in caches:
        copy.wait()
    m1, l1, o1 = attend(own_q, kk, vv, bias[0])
    qcopy.wait_recv()
    m2, l2, o2 = attend(qrecv[...], kk, vv, bias[1])
    psend[pl.ds(0, 2 * ROWS), :] = o2
    wide_lane = lax.broadcasted_iota(jnp.int32, (2 * ROWS, HD), 1)
    psend[pl.ds(2 * ROWS, 2 * ROWS), :] = jnp.where(wide_lane < HD // 2, m2, l2)
    pcopy = pltpu.make_async_remote_copy(
        src_ref=psend,
        dst_ref=precv,
        send_sem=p_sem.at[0],
        recv_sem=p_sem.at[1],
        device_id={"req": partner},
        device_id_type=pl.DeviceIdType.MESH,
    )
    pcopy.start()
    for k in FAR + (0,):
        outw[k].wait()
    pcopy.wait_recv()
    o3 = precv[pl.ds(0, 2 * ROWS), :]
    stats = precv[pl.ds(2 * ROWS, 2 * ROWS), :]
    m3 = stats[:, :1]
    l3 = stats[:, HD // 2 : HD // 2 + 1]
    top = jnp.maximum(m1, m3)
    e1 = jnp.exp(m1 - top)
    e3 = jnp.exp(m3 - top)
    context = ((o1 * e1 + o3 * e3) / (l1 * e1 + l3 * e3)).astype(bf16)
    context = jnp.concatenate([context[:ROWS], context[ROWS:]], axis=1)

    ocopy = {}
    for k in FAR:
        osend[k] = jnp.dot(context, wov[k], preferred_element_type=f32).astype(bf16)
        ocopy[k] = pltpu.make_async_remote_copy(
            src_ref=osend.at[k],
            dst_ref=orecv.at[k],
            send_sem=os_sem.at[k],
            recv_sem=or_sem.at[k],
            device_id={"tp": peer[k]},
            device_id_type=pl.DeviceIdType.MESH,
        )
        ocopy[k].start()
    total = jnp.dot(context, wov[0], preferred_element_type=f32)
    for k in NEAR:
        ocopy[k].wait_recv()
        total = total + orecv[k].astype(f32)
    total = total.astype(bf16)
    for s in range(STEPS):
        out[s] = total[s * OWN : (s + 1) * OWN]
    for k in NEAR:
        xcopy[k].wait_send()
    qcopy.wait_send()
    pcopy.wait_send()
    for k in NEAR:
        ocopy[k].wait_send()


def body(
    hidden_in, norm_gain, w_query, w_key, w_value, w_out,
    prompt_keys, prompt_values, gen_keys, gen_values, lengths, parents,
):
    dma = pltpu.SemaphoreType.DMA
    anywhere = pl.BlockSpec(memory_space=pltpu.HBM)
    return pl.pallas_call(
        kernel,
        out_shape=jax.ShapeDtypeStruct((STEPS, OWN, BLK), bf16),
        in_specs=[anywhere] * 12,
        out_specs=pl.BlockSpec(memory_space=pltpu.VMEM),
        scratch_shapes=[
            pltpu.VMEM((STEPS, OWN, BLK), bf16),
            pltpu.VMEM((ROWS, BLK), bf16),
            pltpu.VMEM((TP, ROWS, BLK), bf16),
            pltpu.VMEM((TP, 1, BLK), f32),
            pltpu.VMEM((TP, BLK, 2 * HD), bf16),
            pltpu.VMEM((TP, BLK, HD), bf16),
            pltpu.VMEM((TP, BLK, HD), bf16),
            pltpu.VMEM((TP, 2 * HD, BLK), bf16),
            pltpu.VMEM((KEYS, HD), bf16),
            pltpu.VMEM((KEYS, HD), bf16),
            pltpu.SMEM((32,), jnp.int32),
            pltpu.SMEM((STEPS, 256), jnp.int32),
            pltpu.VMEM((2, 2 * ROWS, KEYS), f32),
            pltpu.VMEM((2 * ROWS, HD), bf16),
            pltpu.VMEM((2 * ROWS, HD), bf16),
            pltpu.VMEM((4 * ROWS, HD), f32),
            pltpu.VMEM((4 * ROWS, HD), f32),
            pltpu.VMEM((TP, ROWS, BLK), bf16),
            pltpu.VMEM((TP, ROWS, BLK), bf16),
            dma((6,)), dma((TP,)), dma((TP,)), dma((TP,)), dma((TP,)), dma((OWN,)), dma((OWN,)),
            dma((TP,)), dma((TP,)), dma((2,)), dma((2,)), dma((TP,)), dma((TP,)),
        ],
        compiler_params=pltpu.CompilerParams(
            collective_id=0, has_side_effects=True, vmem_limit_bytes=32 * 2**20
        ),
        name="decode_block",
    )(
        hidden_in,
        norm_gain.reshape(TP, 1, BLK),
        w_query,
        w_key,
        w_value,
        w_out,
        prompt_keys.reshape(HALF, HD),
        prompt_values.reshape(HALF, HD),
        gen_keys,
        gen_values,
        lengths,
        parents,
    )


def solution(mesh):
    in_specs = (
        P(None, "req", "tp"),
        P(),
        P(None, "tp"),
        P(None, "tp"),
        P(None, "tp"),
        P("tp", None),
        P("req", None, "tp"),
        P("req", None, "tp"),
        P("req", None, "tp"),
        P("req", None, "tp"),
        P(),
        P(),
    )
    out_specs = P(None, "req", "tp")
    return jax.shard_map(body, mesh=mesh, in_specs=in_specs, out_specs=out_specs, check_vma=False)
```

```python
import math

import jax
import jax.numpy as jnp
from jax import lax
from jax.experimental import pallas as pl
from jax.experimental.pallas import tpu as pltpu
from jax.sharding import PartitionSpec as P

HD = 128
TP = 8
STEPS = 4
OWN = 4
BEAMS = 8
ROWS = STEPS * OWN
BLK = 384
D = TP * BLK
HALF = 512
GEN = 64
KEYS = HALF + OWN * GEN + 128
NEW = HALF + OWN * GEN
EPS = 1e-05
NEG = -1e30
ROPE_BASE = 500000.0
NEAR = (1, 2, 3, 6, 7, 4, 5)
FAR = (4, 5, 2, 3, 6, 7, 1)

bf16 = jnp.bfloat16
f32 = jnp.float32


def flip(index, k):
    result = 0
    for bit in (1, 2, 4):
        digit = (index // bit) % 2
        result += bit * ((1 - digit) if k & bit else digit)
    return result


def attend(q, kk, vv, bias):
    s = lax.dot_general(q, kk[...], (((1,), (1,)), ((), ())), preferred_element_type=f32)
    s = s * (HD**-0.5) + bias
    m = jnp.max(s, axis=-1, keepdims=True)
    p = jnp.exp(s - m)
    l = jnp.sum(p, axis=-1, keepdims=True)
    o = jnp.dot(p.astype(bf16), vv[...], preferred_element_type=f32)
    return m, l, o


def kernel(
    hidden, gain, wq, wk, wv, wo, pk, pv, gk, gv, lengths, parents,
    out,
    xin, xsend, xbuf, gainv, wqv, wkv, wvv, wov, kk, vv, lens, par, bias,
    qsend, qrecv, psend, precv, osend, orecv,
    in_sem, wq_sem, wk_sem, wv_sem, wo_sem, gk_sem, gv_sem,
    xs_sem, xr_sem, q_sem, p_sem, os_sem, or_sem,
):
    req = lax.axis_index("req")
    tp = lax.axis_index("tp")
    parity = req % 2
    request = req // 2
    partner = req + 1 - 2 * parity
    peer = [flip(tp, k) for k in range(TP)]

    local = [
        pltpu.make_async_copy(hidden, xin, in_sem.at[0]),
        pltpu.make_async_copy(gain, gainv, in_sem.at[1]),
        pltpu.make_async_copy(lengths, lens, in_sem.at[2]),
        pltpu.make_async_copy(parents, par, in_sem.at[3]),
        pltpu.make_async_copy(pk, kk.at[pl.ds(0, HALF)], in_sem.at[4]),
        pltpu.make_async_copy(pv, vv.at[pl.ds(0, HALF)], in_sem.at[5]),
    ]
    local[0].start()

    barrier = pltpu.get_barrier_semaphore()
    for k in range(1, TP):
        pl.semaphore_signal(
            barrier, inc=1, device_id={"tp": peer[k]}, device_id_type=pl.DeviceIdType.MESH
        )
    pl.semaphore_signal(
        barrier, inc=1, device_id={"req": partner}, device_id_type=pl.DeviceIdType.MESH
    )

    for copy in local[1:4]:
        copy.start()
    weights = []
    for k in (0,) + NEAR:
        rows = pl.ds(pl.multiple_of(peer[k] * BLK, BLK), BLK)
        mine = [
            pltpu.make_async_copy(wq.at[rows], wqv.at[k], wq_sem.at[k]),
            pltpu.make_async_copy(wk.at[rows], wkv.at[k], wk_sem.at[k]),
            pltpu.make_async_copy(wv.at[rows], wvv.at[k], wv_sem.at[k]),
        ]
        for copy in mine:
            copy.start()
        weights.append(mine)

    local[0].wait()
    x = xin[...].astype(f32)
    x = jnp.concatenate([x[s] for s in range(STEPS)], axis=0)
    xsend[...] = x.astype(bf16)
    pl.semaphore_wait(barrier, TP)
    xcopy = {}
    for k in FAR:
        xcopy[k] = pltpu.make_async_remote_copy(
            src_ref=xsend,
            dst_ref=xbuf.at[k],
            send_sem=xs_sem.at[k],
            recv_sem=xr_sem.at[k],
            device_id={"tp": peer[k]},
            device_id_type=pl.DeviceIdType.MESH,
        )
        xcopy[k].start()

    local[4].start()
    local[5].start()
    caches = []
    for b in range(OWN):
        there = pl.ds(HALF + b * GEN, GEN)
        caches.append(pltpu.make_async_copy(gk.at[b], kk.at[there], gk_sem.at[b]))
        caches.append(pltpu.make_async_copy(gv.at[b], vv.at[there], gv_sem.at[b]))
    for copy in caches:
        copy.start()
    outw = {}
    for k in FAR + (0,):
        cols = pl.ds(pl.multiple_of(peer[k] * BLK, BLK), BLK)
        outw[k] = pltpu.make_async_copy(wo.at[:, cols], wov.at[k], wo_sem.at[k])
        outw[k].start()

    local[2].wait()
    local[3].wait()
    length = lens[request]
    row = lax.broadcasted_iota(jnp.int32, (ROWS, HD), 0)
    lane = lax.broadcasted_iota(jnp.int32, (ROWS, HD), 1)
    position = (length + GEN + row // OWN).astype(f32)
    frequency = jnp.exp((lane % (HD // 2)).astype(f32) * (-math.log(ROPE_BASE) / (HD // 2)))
    angle = position * frequency
    cosine = jnp.cos(angle)
    sine = jnp.sin(angle)
    sine = jnp.where(lane < HD // 2, -sine, sine)

    wide = lax.broadcasted_iota(jnp.int32, (ROWS, HALF), 1)
    prompt_bias = jnp.where(parity * HALF + wide < length, 0.0, NEG).astype(f32)
    gen_beam = OWN * parity + lax.broadcasted_iota(jnp.int32, (ROWS, OWN * GEN), 1) // GEN
    zero = jnp.zeros((128, HD), bf16)
    kk[pl.ds(NEW, 128), :] = zero
    vv[pl.ds(NEW, 128), :] = zero
    for side in range(2):
        first = OWN * (parity if side == 0 else 1 - parity)
        gen_from = jnp.zeros((ROWS, HD), jnp.int32)
        new_from = jnp.full((ROWS, HD), -1, jnp.int32)
        for s in range(STEPS):
            for b in range(OWN):
                here = row == s * OWN + b
                at = first + b
                for t in range(s, -1, -1):
                    new_from = jnp.where(here & (lane // OWN == t), at, new_from)
                    at = par[t, request * BEAMS + at]
                gen_from = jnp.where(here, at, gen_from)
        gen_from = jnp.concatenate([gen_from, gen_from], axis=1)
        gen_bias = jnp.where(gen_from == gen_beam, 0.0, NEG).astype(f32)
        new_bias = jnp.where(new_from == OWN * parity + lane % OWN, 0.0, NEG).astype(f32)
        table = jnp.concatenate([prompt_bias, gen_bias, new_bias], axis=1)
        bias[side, pl.ds(0, ROWS), :] = table
        bias[side, pl.ds(ROWS, ROWS), :] = table

    local[1].wait()
    acc_q = jnp.zeros((ROWS, 2 * HD), f32)
    acc_k = jnp.zeros((ROWS, HD), f32)
    acc_v = jnp.zeros((ROWS, HD), f32)
    squares = jnp.zeros((ROWS, HD), f32)
    for i, k in enumerate((0,) + NEAR):
        if k:
            xcopy[k].wait_recv()
            x = xbuf[k].astype(f32)
        for copy in weights[i]:
            copy.wait()
        for c in range(BLK // HD):
            part = x[:, c * HD : (c + 1) * HD]
            squares = squares + part * part
        scaled = (x * gainv[peer[k]]).astype(bf16)
        acc_q = acc_q + jnp.dot(scaled, wqv[k], preferred_element_type=f32)
        acc_k = acc_k + jnp.dot(scaled, wkv[k], preferred_element_type=f32)
        acc_v = acc_v + jnp.dot(scaled, wvv[k], preferred_element_type=f32)
    inverse = lax.rsqrt(jnp.sum(squares, axis=-1, keepdims=True) / D + EPS)

    def rotated(value):
        value = value * inverse
        return (value * cosine + pltpu.roll(value, HD // 2, 1) * sine).astype(bf16)

    own_q = jnp.concatenate([rotated(acc_q[:, :HD]), rotated(acc_q[:, HD:])], axis=0)
    qsend[...] = own_q
    qcopy = pltpu.make_async_remote_copy(
        src_ref=qsend,
        dst_ref=qrecv,
        send_sem=q_sem.at[0],
        recv_sem=q_sem.at[1],
        device_id={"req": partner},
        device_id_type=pl.DeviceIdType.MESH,
    )
    qcopy.start()
    kk[pl.ds(NEW, ROWS), :] = rotated(acc_k)
    vv[pl.ds(NEW, ROWS), :] = (acc_v * inverse).astype(bf16)

    local[4].wait()
    local[5].wait()
    for copy in caches:
        copy.wait()
    m1, l1, o1 = attend(own_q, kk, vv, bias[0])
    qcopy.wait_recv()
    m2, l2, o2 = attend(qrecv[...], kk, vv, bias[1])
    psend[pl.ds(0, 2 * ROWS), :] = o2
    wide_lane = lax.broadcasted_iota(jnp.int32, (2 * ROWS, HD), 1)
    psend[pl.ds(2 * ROWS, 2 * ROWS), :] = jnp.where(wide_lane < HD // 2, m2, l2)
    pcopy = pltpu.make_async_remote_copy(
        src_ref=psend,
        dst_ref=precv,
        send_sem=p_sem.at[0],
        recv_sem=p_sem.at[1],
        device_id={"req": partner},
        device_id_type=pl.DeviceIdType.MESH,
    )
    pcopy.start()
    for k in FAR + (0,):
        outw[k].wait()
    pcopy.wait_recv()
    o3 = precv[pl.ds(0, 2 * ROWS), :]
    stats = precv[pl.ds(2 * ROWS, 2 * ROWS), :]
    m3 = stats[:, :1]
    l3 = stats[:, HD // 2 : HD // 2 + 1]
    top = jnp.maximum(m1, m3)
    e1 = jnp.exp(m1 - top)
    e3 = jnp.exp(m3 - top)
    context = ((o1 * e1 + o3 * e3) / (l1 * e1 + l3 * e3)).astype(bf16)
    context = jnp.concatenate([context[:ROWS], context[ROWS:]], axis=1)

    ocopy = {}
    for k in FAR:
        osend[k] = jnp.dot(context, wov[k], preferred_element_type=f32).astype(bf16)
        ocopy[k] = pltpu.make_async_remote_copy(
            src_ref=osend.at[k],
            dst_ref=orecv.at[k],
            send_sem=os_sem.at[k],
            recv_sem=or_sem.at[k],
            device_id={"tp": peer[k]},
            device_id_type=pl.DeviceIdType.MESH,
        )
        ocopy[k].start()
    total = jnp.dot(context, wov[0], preferred_element_type=f32)
    for k in NEAR:
        ocopy[k].wait_recv()
        total = total + orecv[k].astype(f32)
    total = total.astype(bf16)
    for s in range(STEPS):
        out[s] = total[s * OWN : (s + 1) * OWN]
    for k in NEAR:
        xcopy[k].wait_send()
    qcopy.wait_send()
    pcopy.wait_send()
    for k in NEAR:
        ocopy[k].wait_send()


def body(
    hidden_in, norm_gain, w_query, w_key, w_value, w_out,
    prompt_keys, prompt_values, gen_keys, gen_values, lengths, parents,
):
    operands = [
        hidden_in,
        norm_gain.reshape(TP, 1, BLK),
        w_query,
        w_key,
        w_value,
        w_out,
        prompt_keys.reshape(HALF, HD),
        prompt_values.reshape(HALF, HD),
        gen_keys,
        gen_values,
        lengths,
        parents,
    ]
    dma = pltpu.SemaphoreType.DMA
    anywhere = pl.BlockSpec(memory_space=pltpu.HBM)
    return pl.pallas_call(
        kernel,
        out_shape=jax.ShapeDtypeStruct((STEPS, OWN, BLK), bf16),
        in_specs=[anywhere] * 12,
        out_specs=pl.BlockSpec(memory_space=pltpu.VMEM),
        scratch_shapes=[
            pltpu.VMEM((STEPS, OWN, BLK), bf16),
            pltpu.VMEM((ROWS, BLK), bf16),
            pltpu.VMEM((TP, ROWS, BLK), bf16),
            pltpu.VMEM((TP, 1, BLK), f32),
            pltpu.VMEM((TP, BLK, 2 * HD), bf16),
            pltpu.VMEM((TP, BLK, HD), bf16),
            pltpu.VMEM((TP, BLK, HD), bf16),
            pltpu.VMEM((TP, 2 * HD, BLK), bf16),
            pltpu.VMEM((KEYS, HD), bf16),
            pltpu.VMEM((KEYS, HD), bf16),
            pltpu.SMEM((32,), jnp.int32),
            pltpu.SMEM((STEPS, 256), jnp.int32),
            pltpu.VMEM((2, 2 * ROWS, KEYS), f32),
            pltpu.VMEM((2 * ROWS, HD), bf16),
            pltpu.VMEM((2 * ROWS, HD), bf16),
            pltpu.VMEM((4 * ROWS, HD), f32),
            pltpu.VMEM((4 * ROWS, HD), f32),
            pltpu.VMEM((TP, ROWS, BLK), bf16),
            pltpu.VMEM((TP, ROWS, BLK), bf16),
            dma((6,)), dma((TP,)), dma((TP,)), dma((TP,)), dma((TP,)), dma((OWN,)), dma((OWN,)),
            dma((TP,)), dma((TP,)), dma((2,)), dma((2,)), dma((TP,)), dma((TP,)),
        ],
        compiler_params=pltpu.CompilerParams(
            collective_id=0, has_side_effects=True, vmem_limit_bytes=24 * 2**20
        ),
        name="decode_block",
    )(*[pltpu.with_memory_space_constraint(x, pltpu.HBM) for x in operands])


def solution(mesh):
    in_specs = (
        P(None, "req", "tp"),
        P(),
        P(None, "tp"),
        P(None, "tp"),
        P(None, "tp"),
        P("tp", None),
        P("req", None, "tp"),
        P("req", None, "tp"),
        P("req", None, "tp"),
        P("req", None, "tp"),
        P(),
        P(),
    )
    out_specs = P(None, "req", "tp")
    return jax.shard_map(body, mesh=mesh, in_specs=in_specs, out_specs=out_specs, check_vma=False)
```

```python
import math

import jax
import jax.numpy as jnp
from jax import lax
from jax.experimental import pallas as pl
from jax.experimental.pallas import tpu as pltpu
from jax.sharding import PartitionSpec as P

HD = 128
TP = 8
STEPS = 4
OWN = 4
BEAMS = 8
ROWS = STEPS * OWN
BLK = 384
D = TP * BLK
HALF = 512
GEN = 64
KEYS = HALF + OWN * GEN + 128
NEW = HALF + OWN * GEN
EPS = 1e-05
NEG = -1e30
ROPE_BASE = 500000.0
GROUP = 2 * TP
FAR_GROUP = (12, 13, 4, 5, 10, 11, 14, 15, 2, 3, 6, 7, 8, 9, 1)
FAR = (4, 5, 2, 3, 6, 7, 1)
NEAR = (1, 2, 3, 6, 7, 4, 5)

bf16 = jnp.bfloat16
f32 = jnp.float32


def flip(index, k):
    result = 0
    for bit in (1, 2, 4, 8):
        digit = (index // bit) % 2
        result += bit * ((1 - digit) if k & bit else digit)
    return result


def kernel(
    hidden, gain, wq, wk, wv, wo, pk, pv, gk, gv, lengths, parents,
    out,
    xin, xbuf, xw, gainv, wqv, wkv, wvv, wov, kk, vv, lens, par, bias,
    part, precv, osend, orecv,
    in_sem, w_sem, wo_sem, gk_sem, gv_sem,
    xs_sem, xr_sem, f_sem, p_sem, os_sem, or_sem,
):
    req = lax.axis_index("req")
    tp = lax.axis_index("tp")
    parity = req % 2
    request = req // 2
    me = parity * TP + tp
    member = [flip(me, k) for k in range(GROUP)]

    def device(k):
        there = {}
        if k % TP:
            there["tp"] = member[k] % TP
        if k >= TP:
            there["req"] = req + 1 - 2 * parity
        return there

    def remote(src, dst, send, recv, k):
        return pltpu.make_async_remote_copy(
            src_ref=src, dst_ref=dst, send_sem=send, recv_sem=recv,
            device_id=device(k), device_id_type=pl.DeviceIdType.MESH,
        )

    local = [
        pltpu.make_async_copy(hidden, xin, in_sem.at[0]),
        pltpu.make_async_copy(gain, gainv, in_sem.at[1]),
        pltpu.make_async_copy(lengths, lens, in_sem.at[2]),
        pltpu.make_async_copy(parents, par, in_sem.at[3]),
        pltpu.make_async_copy(pk, kk.at[pl.ds(0, HALF)], in_sem.at[4]),
        pltpu.make_async_copy(pv, vv.at[pl.ds(0, HALF)], in_sem.at[5]),
    ]
    local[0].start()

    barrier = pltpu.get_barrier_semaphore()

    @pl.when(me != 0)
    def _():
        for k in FAR_GROUP:
            pl.semaphore_signal(
                barrier, inc=1, device_id=device(k), device_id_type=pl.DeviceIdType.MESH
            )

    local[0].wait()
    x = xin[...].astype(f32)
    x = jnp.concatenate([x[s] for s in range(STEPS)], axis=0)
    xbuf[me] = x.astype(bf16)

    @pl.when(me == 0)
    def _():
        pl.semaphore_wait(barrier, GROUP - 1)

    @pl.when(me != 0)
    def _():
        pl.semaphore_wait(barrier, GROUP - 2)

    xcopy = {}
    for k in FAR_GROUP:
        xcopy[k] = remote(xbuf.at[me], xbuf.at[me], xs_sem.at[k], xr_sem.at[me], k)

        @pl.when(me != k)
        def _():
            xcopy[k].start()

    for copy in local[1:4]:
        copy.start()
    weights = [
        pltpu.make_async_copy(wq.at[pl.ds(0, D // 2)], wqv.at[pl.ds(0, D // 2)], w_sem.at[0]),
        pltpu.make_async_copy(wq.at[pl.ds(D // 2, D // 2)], wqv.at[pl.ds(D // 2, D // 2)], w_sem.at[1]),
        pltpu.make_async_copy(wk, wkv, w_sem.at[2]),
        pltpu.make_async_copy(wv, wvv, w_sem.at[3]),
    ]
    for copy in weights:
        copy.start()
    caches = [local[4], local[5]]
    for b in range(OWN):
        there = pl.ds(HALF + b * GEN, GEN)
        caches.append(pltpu.make_async_copy(gk.at[b], kk.at[there], gk_sem.at[b]))
        caches.append(pltpu.make_async_copy(gv.at[b], vv.at[there], gv_sem.at[b]))
    for copy in caches:
        copy.start()
    outw = {}
    for k in FAR + (0,):
        cols = pl.ds(pl.multiple_of((member[k] % TP) * BLK, BLK), BLK)
        outw[k] = pltpu.make_async_copy(wo.at[:, cols], wov.at[k], wo_sem.at[k])
        outw[k].start()

    local[2].wait()
    local[3].wait()
    length = lens[request]
    row = lax.broadcasted_iota(jnp.int32, (2 * ROWS, HD), 0)
    lane = lax.broadcasted_iota(jnp.int32, (2 * ROWS, HD), 1)
    position = (length + GEN + (row % ROWS) // OWN).astype(f32)
    frequency = jnp.exp((lane % (HD // 2)).astype(f32) * (-math.log(ROPE_BASE) / (HD // 2)))
    angle = position * frequency
    cosine = jnp.cos(angle)
    sine = jnp.sin(angle)
    sine = jnp.where(lane < HD // 2, -sine, sine)

    wide = lax.broadcasted_iota(jnp.int32, (2 * ROWS, HALF), 1)
    prompt_bias = jnp.where(parity * HALF + wide < length, 0.0, NEG).astype(f32)
    gen_beam = OWN * parity + lax.broadcasted_iota(jnp.int32, (2 * ROWS, OWN * GEN), 1) // GEN
    gen_from = jnp.zeros((2 * ROWS, HD), jnp.int32)
    new_from = jnp.full((2 * ROWS, HD), -1, jnp.int32)
    for half in range(2):
        for s in range(STEPS):
            for b in range(OWN):
                here = row == half * ROWS + s * OWN + b
                at = half * OWN + b
                for t in range(s, -1, -1):
                    new_from = jnp.where(here & ((lane % ROWS) // OWN == t), at, new_from)
                    at = par[t, request * BEAMS + at]
                gen_from = jnp.where(here, at, gen_from)
    gen_from = jnp.concatenate([gen_from, gen_from], axis=1)
    gen_bias = jnp.where(gen_from == gen_beam, 0.0, NEG).astype(f32)
    owned = lane // ROWS == parity
    new_bias = jnp.where(owned & (new_from == OWN * parity + lane % OWN), 0.0, NEG).astype(f32)
    bias[...] = jnp.concatenate([prompt_bias, gen_bias, new_bias], axis=1)
    zero = jnp.zeros((128, HD), bf16)
    kk[pl.ds(NEW, 128), :] = zero
    vv[pl.ds(NEW, 128), :] = zero

    def arrived(k):
        remote(xbuf.at[me], xbuf.at[member[k]], xs_sem.at[k], xr_sem.at[member[k]], k).wait_recv()

    rest = pl.ds(1, GROUP - 1)
    hand = remote(xbuf.at[rest], xbuf.at[rest], f_sem.at[0], f_sem.at[1], 1)

    @pl.when(me == 0)
    def _():
        hand.wait_recv()

    @pl.when(me != 0)
    def _():
        for k in range(1, GROUP):

            @pl.when(me != k)
            def _():
                arrived(k)

    @pl.when(me == 1)
    def _():
        arrived(1)
        hand.start()

    local[1].wait()
    squares = jnp.zeros((2 * ROWS, HD), f32)

    def scaled(j, squares):
        x = jnp.concatenate([xbuf[j].astype(f32), xbuf[TP + j].astype(f32)], axis=0)
        for c in range(BLK // HD):
            piece = x[:, c * HD : (c + 1) * HD]
            squares = squares + piece * piece
        xw[:, j * BLK : (j + 1) * BLK] = (x * gainv[j]).astype(bf16)
        return squares

    for j in range(1, TP):
        squares = scaled(j, squares)
    for copy in weights:
        copy.wait()
    tail = xw[:, BLK:]
    acc_q = jnp.dot(tail, wqv[pl.ds(BLK, D - BLK), :], preferred_element_type=f32)
    acc_k = jnp.dot(tail, wkv[pl.ds(BLK, D - BLK), :], preferred_element_type=f32)
    acc_v = jnp.dot(tail, wvv[pl.ds(BLK, D - BLK), :], preferred_element_type=f32)

    for k in range(2, GROUP):

        @pl.when(me == k)
        def _():
            arrived(k)

    squares = scaled(0, squares)
    head = xw[:, :BLK]
    acc_q = acc_q + jnp.dot(head, wqv[pl.ds(0, BLK), :], preferred_element_type=f32)
    acc_k = acc_k + jnp.dot(head, wkv[pl.ds(0, BLK), :], preferred_element_type=f32)
    acc_v = acc_v + jnp.dot(head, wvv[pl.ds(0, BLK), :], preferred_element_type=f32)
    inverse = lax.rsqrt(jnp.sum(squares, axis=-1, keepdims=True) / D + EPS)

    def rotated(value):
        value = value * inverse
        return (value * cosine + pltpu.roll(value, HD // 2, 1) * sine).astype(bf16)

    q = jnp.concatenate([rotated(acc_q[:, :HD]), rotated(acc_q[:, HD:])], axis=0)
    kk[pl.ds(NEW, 2 * ROWS), :] = rotated(acc_k)
    vv[pl.ds(NEW, 2 * ROWS), :] = (acc_v * inverse).astype(bf16)
    for copy in caches:
        copy.wait()

    s = lax.dot_general(q, kk[...], (((1,), (1,)), ((), ())), preferred_element_type=f32)
    table = bias[...]
    s = s * (HD**-0.5) + jnp.concatenate([table, table], axis=0)
    m = jnp.max(s, axis=-1, keepdims=True)
    p = jnp.exp(s - m)
    l = jnp.sum(p, axis=-1, keepdims=True)
    o = jnp.dot(p.astype(bf16), vv[...], preferred_element_type=f32)
    stats = jnp.where(lax.broadcasted_iota(jnp.int32, (4 * ROWS, HD), 1) < HD // 2, m, l)
    for half in range(2):
        for h in range(2):
            rows = slice((2 * h + half) * ROWS, (2 * h + half + 1) * ROWS)
            part[half, h * ROWS : (h + 1) * ROWS] = o[rows]
            part[half, (2 + h) * ROWS : (3 + h) * ROWS] = stats[rows]
    pcopy = remote(part.at[1 - parity], precv, p_sem.at[0], p_sem.at[1], TP)
    pcopy.start()
    for k in FAR + (0,):
        outw[k].wait()
    mine = part[parity]
    o1, m1, l1 = mine[: 2 * ROWS], mine[2 * ROWS :, :1], mine[2 * ROWS :, HD // 2 : HD // 2 + 1]
    pcopy.wait_recv()
    other = precv[...]
    o2, m2, l2 = other[: 2 * ROWS], other[2 * ROWS :, :1], other[2 * ROWS :, HD // 2 : HD // 2 + 1]
    top = jnp.maximum(m1, m2)
    e1 = jnp.exp(m1 - top)
    e2 = jnp.exp(m2 - top)
    context = ((o1 * e1 + o2 * e2) / (l1 * e1 + l2 * e2)).astype(bf16)
    context = jnp.concatenate([context[:ROWS], context[ROWS:]], axis=1)

    ocopy = {}
    for k in FAR:
        osend[k] = jnp.dot(context, wov[k], preferred_element_type=f32).astype(bf16)
        ocopy[k] = remote(osend.at[k], orecv.at[k], os_sem.at[k], or_sem.at[k], k)
        ocopy[k].start()
    total = jnp.dot(context, wov[0], preferred_element_type=f32)
    for k in NEAR:
        ocopy[k].wait_recv()
        total = total + orecv[k].astype(f32)
    total = total.astype(bf16)
    for s in range(STEPS):
        out[s] = total[s * OWN : (s + 1) * OWN]

    for k in FAR_GROUP:

        @pl.when(me != k)
        def _():
            xcopy[k].wait_send()

    @pl.when(me == 1)
    def _():
        hand.wait_send()

    pcopy.wait_send()
    for k in NEAR:
        ocopy[k].wait_send()


def body(
    hidden_in, norm_gain, w_query, w_key, w_value, w_out,
    prompt_keys, prompt_values, gen_keys, gen_values, lengths, parents,
):
    operands = [
        hidden_in,
        norm_gain.reshape(TP, 1, BLK),
        w_query,
        w_key,
        w_value,
        w_out,
        prompt_keys.reshape(HALF, HD),
        prompt_values.reshape(HALF, HD),
        gen_keys,
        gen_values,
        lengths,
        parents,
    ]
    dma = pltpu.SemaphoreType.DMA
    anywhere = pl.BlockSpec(memory_space=pltpu.HBM)
    return pl.pallas_call(
        kernel,
        out_shape=jax.ShapeDtypeStruct((STEPS, OWN, BLK), bf16),
        in_specs=[anywhere] * 12,
        out_specs=pl.BlockSpec(memory_space=pltpu.VMEM),
        scratch_shapes=[
            pltpu.VMEM((STEPS, OWN, BLK), bf16),
            pltpu.VMEM((GROUP, ROWS, BLK), bf16),
            pltpu.VMEM((2 * ROWS, D), bf16),
            pltpu.VMEM((TP, 1, BLK), f32),
            pltpu.VMEM((D, 2 * HD), bf16),
            pltpu.VMEM((D, HD), bf16),
            pltpu.VMEM((D, HD), bf16),
            pltpu.VMEM((TP, 2 * HD, BLK), bf16),
            pltpu.VMEM((KEYS, HD), bf16),
            pltpu.VMEM((KEYS, HD), bf16),
            pltpu.SMEM((32,), jnp.int32),
            pltpu.SMEM((STEPS, 256), jnp.int32),
            pltpu.VMEM((2 * ROWS, KEYS), f32),
            pltpu.VMEM((2, 4 * ROWS, HD), f32),
            pltpu.VMEM((4 * ROWS, HD), f32),
            pltpu.VMEM((TP, ROWS, BLK), bf16),
            pltpu.VMEM((TP, ROWS, BLK), bf16),
            dma((6,)), dma((4,)), dma((TP,)), dma((OWN,)), dma((OWN,)),
            dma((GROUP,)), dma((GROUP,)), dma((2,)), dma((2,)), dma((TP,)), dma((TP,)),
        ],
        compiler_params=pltpu.CompilerParams(
            collective_id=0, has_side_effects=True, vmem_limit_bytes=24 * 2**20
        ),
        name="decode_block",
    )(*[pltpu.with_memory_space_constraint(x, pltpu.HBM) for x in operands])


def solution(mesh):
    in_specs = (
        P(None, "req", "tp"),
        P(),
        P(None, "tp"),
        P(None, "tp"),
        P(None, "tp"),
        P("tp", None),
        P("req", None, "tp"),
        P("req", None, "tp"),
        P("req", None, "tp"),
        P("req", None, "tp"),
        P(),
        P(),
    )
    out_specs = P(None, "req", "tp")
    return jax.shard_map(body, mesh=mesh, in_specs=in_specs, out_specs=out_specs, check_vma=False)
```

```python
import math

import jax
import jax.numpy as jnp
from jax import lax
from jax.experimental import pallas as pl
from jax.experimental.pallas import tpu as pltpu
from jax.sharding import PartitionSpec as P

HD = 128
TP = 8
STEPS = 4
OWN = 4
BEAMS = 8
ROWS = STEPS * OWN
BLK = 384
D = TP * BLK
HALF = 512
GEN = 64
KEYS = HALF + OWN * GEN + 128
NEW = HALF + OWN * GEN
EPS = 1e-05
NEG = -1e30
ROPE_BASE = 500000.0
GROUP = 2 * TP
FAR_GROUP = (12, 13, 4, 5, 1, 10, 11, 14, 15, 2, 3, 6, 7, 8, 9)
FAR = (4, 5, 2, 3, 6, 7, 1)

bf16 = jnp.bfloat16
f32 = jnp.float32


def flip(index, k):
    result = 0
    for bit in (1, 2, 4, 8):
        digit = (index // bit) % 2
        result += bit * ((1 - digit) if k & bit else digit)
    return result


def kernel(
    hidden, gain, wq, wk, wv, wo, pk, pv, gk, gv, lengths, parents,
    out,
    xbuf, xw, gainv, wqv, wkv, wvv, wov, kk, vv, lens, par, bias,
    part, kept, precv, osend, orecv,
    in_sem, w_sem, wo_sem, gk_sem, gv_sem,
    xs_sem, xr_sem, f_sem, p_sem, os_sem, or_sem,
):
    req = lax.axis_index("req")
    tp = lax.axis_index("tp")
    parity = req % 2
    request = req // 2
    me = parity * TP + tp
    member = [flip(me, k) for k in range(GROUP)]

    def device(k):
        there = {}
        if k % TP:
            there["tp"] = member[k] % TP
        if k >= TP:
            there["req"] = req + 1 - 2 * parity
        return there

    def remote(src, dst, send, recv, k):
        return pltpu.make_async_remote_copy(
            src_ref=src, dst_ref=dst, send_sem=send, recv_sem=recv,
            device_id=device(k), device_id_type=pl.DeviceIdType.MESH,
        )

    local = [
        pltpu.make_async_copy(hidden, xbuf.at[me], in_sem.at[0]),
        pltpu.make_async_copy(gain, gainv, in_sem.at[1]),
        pltpu.make_async_copy(lengths, lens, in_sem.at[2]),
        pltpu.make_async_copy(parents, par, in_sem.at[3]),
        pltpu.make_async_copy(pk, kk.at[pl.ds(0, HALF)], in_sem.at[4]),
        pltpu.make_async_copy(pv, vv.at[pl.ds(0, HALF)], in_sem.at[5]),
    ]
    barrier = pltpu.get_barrier_semaphore()

    @pl.when(me != 0)
    def _():
        for k in FAR_GROUP:
            pl.semaphore_signal(
                barrier, inc=1, device_id=device(k), device_id_type=pl.DeviceIdType.MESH
            )

    @pl.when(me == 0)
    def _():
        pl.semaphore_wait(barrier, GROUP - 1)

    @pl.when(me != 0)
    def _():
        pl.semaphore_wait(barrier, GROUP - 2)

    first = 1 - jnp.minimum(me, 1)
    xcopy = {}
    for k in FAR_GROUP:
        xcopy[k] = remote(hidden, xbuf.at[me], xs_sem.at[0], xr_sem.at[first], k)

        @pl.when(me != k)
        def _():
            xcopy[k].start()

    for copy in local[:4]:
        copy.start()
    weights = [
        pltpu.make_async_copy(wq.at[pl.ds(0, D // 2)], wqv.at[pl.ds(0, D // 2)], w_sem.at[0]),
        pltpu.make_async_copy(wq.at[pl.ds(D // 2, D // 2)], wqv.at[pl.ds(D // 2, D // 2)], w_sem.at[1]),
        pltpu.make_async_copy(wk, wkv, w_sem.at[2]),
        pltpu.make_async_copy(wv, wvv, w_sem.at[3]),
    ]
    for copy in weights:
        copy.start()
    caches = [local[4], local[5]]
    for b in range(OWN):
        there = pl.ds(HALF + b * GEN, GEN)
        caches.append(pltpu.make_async_copy(gk.at[b], kk.at[there], gk_sem.at[b]))
        caches.append(pltpu.make_async_copy(gv.at[b], vv.at[there], gv_sem.at[b]))
    for copy in caches:
        copy.start()
    outw = {}
    for k in FAR + (0,):
        cols = pl.ds(pl.multiple_of((member[k] % TP) * BLK, BLK), BLK)
        outw[k] = pltpu.make_async_copy(wo.at[:, cols], wov.at[k], wo_sem.at[k])
        outw[k].start()

    local[2].wait()
    local[3].wait()
    length = lens[request]
    row = lax.broadcasted_iota(jnp.int32, (2 * ROWS, HD), 0)
    lane = lax.broadcasted_iota(jnp.int32, (2 * ROWS, HD), 1)
    position = (length + GEN + (row % ROWS) // OWN).astype(f32)
    frequency = jnp.exp((lane % (HD // 2)).astype(f32) * (-math.log(ROPE_BASE) / (HD // 2)))
    angle = position * frequency
    cosine = jnp.cos(angle)
    sine = jnp.sin(angle)
    sine = jnp.where(lane < HD // 2, -sine, sine)

    wide = lax.broadcasted_iota(jnp.int32, (2 * ROWS, HALF), 1)
    prompt_bias = jnp.where(parity * HALF + wide < length, 0.0, NEG).astype(f32)
    gen_beam = OWN * parity + lax.broadcasted_iota(jnp.int32, (2 * ROWS, OWN * GEN), 1) // GEN
    gen_from = jnp.zeros((2 * ROWS, HD), jnp.int32)
    new_from = jnp.full((2 * ROWS, HD), -1, jnp.int32)
    for half in range(2):
        for s in range(STEPS):
            for b in range(OWN):
                here = row == half * ROWS + s * OWN + b
                at = half * OWN + b
                for t in range(s, -1, -1):
                    new_from = jnp.where(here & ((lane % ROWS) // OWN == t), at, new_from)
                    at = par[t, request * BEAMS + at]
                gen_from = jnp.where(here, at, gen_from)
    gen_from = jnp.concatenate([gen_from, gen_from], axis=1)
    gen_bias = jnp.where(gen_from == gen_beam, 0.0, NEG).astype(f32)
    owned = lane // ROWS == parity
    new_bias = jnp.where(owned & (new_from == OWN * parity + lane % OWN), 0.0, NEG).astype(f32)
    bias[...] = jnp.concatenate([prompt_bias, gen_bias, new_bias], axis=1)
    zero = jnp.zeros((128, HD), bf16)
    kk[pl.ds(NEW, 128), :] = zero
    vv[pl.ds(NEW, 128), :] = zero

    def blocks(count, sem):
        some = xbuf.at[pl.ds(0, count)]
        return pltpu.make_async_copy(some, some, sem)

    rest = pl.ds(1, GROUP - 1)
    hand = remote(xbuf.at[rest], xbuf.at[rest], f_sem.at[0], f_sem.at[1], 1)
    local[0].wait()

    @pl.when(me == 0)
    def _():
        hand.wait_recv()

    @pl.when(me != 0)
    def _():
        blocks(GROUP - 2, xr_sem.at[0]).wait()

    @pl.when(me == 1)
    def _():
        blocks(1, xr_sem.at[1]).wait()
        hand.start()

    local[1].wait()
    squares = jnp.zeros((2 * ROWS, HD), f32)

    def scaled(j, squares):
        x = jnp.concatenate(
            [xbuf[i, s].astype(f32) for i in (j, TP + j) for s in range(STEPS)], axis=0
        )
        for c in range(BLK // HD):
            piece = x[:, c * HD : (c + 1) * HD]
            squares = squares + piece * piece
        xw[:, j * BLK : (j + 1) * BLK] = (x * gainv[j]).astype(bf16)
        return squares

    for j in range(1, TP):
        squares = scaled(j, squares)
    for copy in weights:
        copy.wait()
    tail = xw[:, BLK:]
    acc_q = jnp.dot(tail, wqv[pl.ds(BLK, D - BLK), :], preferred_element_type=f32)
    acc_k = jnp.dot(tail, wkv[pl.ds(BLK, D - BLK), :], preferred_element_type=f32)
    acc_v = jnp.dot(tail, wvv[pl.ds(BLK, D - BLK), :], preferred_element_type=f32)

    @pl.when(me > 1)
    def _():
        blocks(1, xr_sem.at[1]).wait()

    squares = scaled(0, squares)
    head = xw[:, :BLK]
    acc_q = acc_q + jnp.dot(head, wqv[pl.ds(0, BLK), :], preferred_element_type=f32)
    acc_k = acc_k + jnp.dot(head, wkv[pl.ds(0, BLK), :], preferred_element_type=f32)
    acc_v = acc_v + jnp.dot(head, wvv[pl.ds(0, BLK), :], preferred_element_type=f32)
    inverse = lax.rsqrt(jnp.sum(squares, axis=-1, keepdims=True) / D + EPS)

    def rotated(value):
        value = value * inverse
        return (value * cosine + pltpu.roll(value, HD // 2, 1) * sine).astype(bf16)

    q = jnp.concatenate([rotated(acc_q[:, :HD]), rotated(acc_q[:, HD:])], axis=0)
    kk[pl.ds(NEW, 2 * ROWS), :] = rotated(acc_k)
    vv[pl.ds(NEW, 2 * ROWS), :] = (acc_v * inverse).astype(bf16)
    for copy in caches:
        copy.wait()

    s = lax.dot_general(q, kk[...], (((1,), (1,)), ((), ())), preferred_element_type=f32)
    table = bias[...]
    s = s * (HD**-0.5) + jnp.concatenate([table, table], axis=0)
    m = jnp.max(s, axis=-1, keepdims=True)
    p = jnp.exp(s - m)
    l = jnp.sum(p, axis=-1, keepdims=True)
    o = jnp.dot(p.astype(bf16), vv[...], preferred_element_type=f32)
    mixed = m + jnp.log(l)
    o = o / l
    lane4 = lax.broadcasted_iota(jnp.int32, (4 * ROWS, HD), 1)
    high = mixed.astype(bf16).astype(f32)
    middle = (mixed - high).astype(bf16).astype(f32)
    low = mixed - high - middle
    terms = jnp.where(lane4 < HD // 4, high, jnp.where(lane4 < HD // 2, middle, low)).astype(bf16)
    rounded = o.astype(bf16)
    for half in range(2):
        for h in range(2):
            rows = slice((2 * h + half) * ROWS, (2 * h + half + 1) * ROWS)
            part[half, h * ROWS : (h + 1) * ROWS] = rounded[rows]
            part[half, (2 + h) * ROWS : (3 + h) * ROWS] = terms[rows]
    pcopy = remote(part.at[1 - parity], precv, p_sem.at[0], p_sem.at[1], TP)
    pcopy.start()
    for half in range(2):
        for h in range(2):
            rows = slice((2 * h + half) * ROWS, (2 * h + half + 1) * ROWS)
            kept[half, h * ROWS : (h + 1) * ROWS] = o[rows]
            kept[half, (2 + h) * ROWS : (3 + h) * ROWS] = jnp.broadcast_to(mixed, o.shape)[rows]
    for k in FAR + (0,):
        outw[k].wait()

    @pl.when(me == 0)
    def _():
        blocks(GROUP - 1, xs_sem.at[0]).wait()

    @pl.when(me != 0)
    def _():
        blocks(GROUP - 2, xs_sem.at[0]).wait()

    @pl.when(me == 1)
    def _():
        hand.wait_send()

    mine = kept[parity]
    o1, m1 = mine[: 2 * ROWS], mine[2 * ROWS :]
    pcopy.wait_recv()
    other = precv[...].astype(f32)
    o2, terms = other[: 2 * ROWS], other[2 * ROWS :]
    m2 = terms[:, :1] + terms[:, HD // 4 : HD // 4 + 1] + terms[:, HD // 2 : HD // 2 + 1]
    top = jnp.maximum(m1, m2)
    e1 = jnp.exp(m1 - top)
    e2 = jnp.exp(m2 - top)
    context = ((o1 * e1 + o2 * e2) / (e1 + e2)).astype(bf16)
    context = jnp.concatenate([context[:ROWS], context[ROWS:]], axis=1)

    def outputs(ref, sem):
        some = ref.at[pl.ds(1, TP - 1)]
        return pltpu.make_async_copy(some, some, sem)

    for k in FAR:
        osend[k] = jnp.dot(context, wov[k], preferred_element_type=f32).astype(bf16)
        remote(osend.at[k], orecv.at[k], os_sem.at[0], or_sem.at[0], k).start()
    total = jnp.dot(context, wov[0], preferred_element_type=f32)
    pcopy.wait_send()
    outputs(orecv, or_sem.at[0]).wait()
    for k in range(1, TP):
        total = total + orecv[k].astype(f32)
    total = total.astype(bf16)
    for s in range(STEPS):
        out[s] = total[s * OWN : (s + 1) * OWN]

    outputs(osend, os_sem.at[0]).wait()


def body(
    hidden_in, norm_gain, w_query, w_key, w_value, w_out,
    prompt_keys, prompt_values, gen_keys, gen_values, lengths, parents,
):
    operands = [
        hidden_in,
        norm_gain.reshape(TP, 1, BLK),
        w_query,
        w_key,
        w_value,
        w_out,
        prompt_keys.reshape(HALF, HD),
        prompt_values.reshape(HALF, HD),
        gen_keys,
        gen_values,
        lengths,
        parents,
    ]
    dma = pltpu.SemaphoreType.DMA
    anywhere = pl.BlockSpec(memory_space=pltpu.HBM)
    return pl.pallas_call(
        kernel,
        out_shape=jax.ShapeDtypeStruct((STEPS, OWN, BLK), bf16),
        in_specs=[anywhere] * 12,
        out_specs=pl.BlockSpec(memory_space=pltpu.VMEM),
        scratch_shapes=[
            pltpu.VMEM((GROUP, STEPS, OWN, BLK), bf16),
            pltpu.VMEM((2 * ROWS, D), bf16),
            pltpu.VMEM((TP, 1, BLK), f32),
            pltpu.VMEM((D, 2 * HD), bf16),
            pltpu.VMEM((D, HD), bf16),
            pltpu.VMEM((D, HD), bf16),
            pltpu.VMEM((TP, 2 * HD, BLK), bf16),
            pltpu.VMEM((KEYS, HD), bf16),
            pltpu.VMEM((KEYS, HD), bf16),
            pltpu.SMEM((32,), jnp.int32),
            pltpu.SMEM((STEPS, 256), jnp.int32),
            pltpu.VMEM((2 * ROWS, KEYS), f32),
            pltpu.VMEM((2, 4 * ROWS, HD), bf16),
            pltpu.VMEM((2, 4 * ROWS, HD), f32),
            pltpu.VMEM((4 * ROWS, HD), bf16),
            pltpu.VMEM((TP, ROWS, BLK), bf16),
            pltpu.VMEM((TP, ROWS, BLK), bf16),
            dma((6,)), dma((4,)), dma((TP,)), dma((OWN,)), dma((OWN,)),
            dma((1,)), dma((2,)), dma((2,)), dma((2,)), dma((1,)), dma((1,)),
        ],
        compiler_params=pltpu.CompilerParams(
            collective_id=0, has_side_effects=True, vmem_limit_bytes=24 * 2**20
        ),
        name="decode_block",
    )(*[pltpu.with_memory_space_constraint(x, pltpu.HBM) for x in operands])


def solution(mesh):
    in_specs = (
        P(None, "req", "tp"),
        P(),
        P(None, "tp"),
        P(None, "tp"),
        P(None, "tp"),
        P("tp", None),
        P("req", None, "tp"),
        P("req", None, "tp"),
        P("req", None, "tp"),
        P("req", None, "tp"),
        P(),
        P(),
    )
    out_specs = P(None, "req", "tp")
    return jax.shard_map(body, mesh=mesh, in_specs=in_specs, out_specs=out_specs, check_vma=False)
```

```python
import math

import jax
import jax.numpy as jnp
from jax import lax
from jax.experimental import pallas as pl
from jax.experimental.pallas import tpu as pltpu
from jax.sharding import PartitionSpec as P

HD = 128
TP = 8
STEPS = 4
OWN = 4
BEAMS = 8
ROWS = STEPS * OWN
BLK = 384
D = TP * BLK
HALF = 512
GEN = 64
KEYS = HALF + OWN * GEN + 128
NEW = HALF + OWN * GEN
EPS = 1e-05
NEG = -1e30
ROPE_BASE = 500000.0
GROUP = 2 * TP
FAR_GROUP = (12, 13, 4, 5, 1, 10, 11, 14, 15, 2, 3, 6, 7, 8, 9)
FAR = (4, 5, 2, 3, 6, 7, 1)

bf16 = jnp.bfloat16
f32 = jnp.float32


def flip(index, k):
    result = 0
    for bit in (1, 2, 4, 8):
        digit = (index // bit) % 2
        result += bit * ((1 - digit) if k & bit else digit)
    return result


def kernel(
    hidden, gain, wq, wk, wv, wo, pk, pv, gk, gv, lengths, parents,
    out,
    xbuf, xw, gainv, wqv, wkv, wvv, wov, kk, vv, lens, par, bias,
    part, kept, precv, osend, orecv,
    in_sem, w_sem, wo_sem, gk_sem, gv_sem,
    xs_sem, xr_sem, f_sem, p_sem, os_sem, or_sem,
):
    req = lax.axis_index("req")
    tp = lax.axis_index("tp")
    parity = req % 2
    request = req // 2
    me = parity * TP + tp
    member = [flip(me, k) for k in range(GROUP)]

    def device(k):
        there = {}
        if k % TP:
            there["tp"] = member[k] % TP
        if k >= TP:
            there["req"] = req + 1 - 2 * parity
        return there

    def remote(src, dst, send, recv, k):
        return pltpu.make_async_remote_copy(
            src_ref=src, dst_ref=dst, send_sem=send, recv_sem=recv,
            device_id=device(k), device_id_type=pl.DeviceIdType.MESH,
        )

    local = [
        pltpu.make_async_copy(hidden, xbuf.at[me], in_sem.at[0]),
        pltpu.make_async_copy(gain, gainv, in_sem.at[1]),
        pltpu.make_async_copy(lengths, lens, in_sem.at[2]),
        pltpu.make_async_copy(parents, par, in_sem.at[3]),
        pltpu.make_async_copy(pk, kk.at[pl.ds(0, HALF)], in_sem.at[4]),
        pltpu.make_async_copy(pv, vv.at[pl.ds(0, HALF)], in_sem.at[5]),
    ]
    barrier = pltpu.get_barrier_semaphore()

    @pl.when(me != 0)
    def _():
        for k in FAR_GROUP:
            pl.semaphore_signal(
                barrier, inc=1, device_id=device(k), device_id_type=pl.DeviceIdType.MESH
            )

    @pl.when(me == 0)
    def _():
        pl.semaphore_wait(barrier, GROUP - 1)

    @pl.when(me != 0)
    def _():
        pl.semaphore_wait(barrier, GROUP - 2)

    first = 1 - jnp.minimum(me, 1)
    xcopy = {}
    for k in FAR_GROUP:
        xcopy[k] = remote(hidden, xbuf.at[me], xs_sem.at[0], xr_sem.at[first], k)

        @pl.when(me != k)
        def _():
            xcopy[k].start()

    for copy in local[:4]:
        copy.start()
    weights = []
    for source, target, pieces in ((wq, wqv, 2), (wk, wkv, 1), (wv, wvv, 1)):
        for piece in range(pieces):
            rows = pl.ds(piece * (D // pieces), D // pieces)
            weights.append(
                pltpu.make_async_copy(source.at[rows], target.at[rows], w_sem.at[len(weights)])
            )
    for copy in weights:
        copy.start()
    caches = [local[4], local[5]]
    for b in range(OWN):
        there = pl.ds(HALF + b * GEN, GEN)
        caches.append(pltpu.make_async_copy(gk.at[b], kk.at[there], gk_sem.at[b]))
        caches.append(pltpu.make_async_copy(gv.at[b], vv.at[there], gv_sem.at[b]))
    for copy in caches:
        copy.start()
    outw = {0: pltpu.make_async_copy(wo, wov, wo_sem.at[0])}
    outw[0].start()

    local[2].wait()
    local[3].wait()
    length = lens[request]
    row = lax.broadcasted_iota(jnp.int32, (2 * ROWS, HD), 0)
    lane = lax.broadcasted_iota(jnp.int32, (2 * ROWS, HD), 1)
    position = (length + GEN + (row % ROWS) // OWN).astype(f32)
    frequency = jnp.exp((lane % (HD // 2)).astype(f32) * (-math.log(ROPE_BASE) / (HD // 2)))
    angle = position * frequency
    cosine = jnp.cos(angle)
    sine = jnp.sin(angle)
    sine = jnp.where(lane < HD // 2, -sine, sine)

    wide = lax.broadcasted_iota(jnp.int32, (2 * ROWS, HALF), 1)
    prompt_bias = jnp.where(parity * HALF + wide < length, 0.0, NEG).astype(f32)
    gen_beam = OWN * parity + lax.broadcasted_iota(jnp.int32, (2 * ROWS, OWN * GEN), 1) // GEN
    gen_from = jnp.zeros((2 * ROWS, HD), jnp.int32)
    new_from = jnp.full((2 * ROWS, HD), -1, jnp.int32)
    for half in range(2):
        for s in range(STEPS):
            for b in range(OWN):
                here = row == half * ROWS + s * OWN + b
                at = half * OWN + b
                for t in range(s, -1, -1):
                    new_from = jnp.where(here & ((lane % ROWS) // OWN == t), at, new_from)
                    at = par[t, request * BEAMS + at]
                gen_from = jnp.where(here, at, gen_from)
    gen_from = jnp.concatenate([gen_from, gen_from], axis=1)
    gen_bias = jnp.where(gen_from == gen_beam, 0.0, NEG).astype(f32)
    owned = lane // ROWS == parity
    new_bias = jnp.where(owned & (new_from == OWN * parity + lane % OWN), 0.0, NEG).astype(f32)
    bias[...] = jnp.concatenate([prompt_bias, gen_bias, new_bias], axis=1)
    zero = jnp.zeros((128, HD), bf16)
    kk[pl.ds(NEW, 128), :] = zero
    vv[pl.ds(NEW, 128), :] = zero

    def blocks(count, sem):
        some = xbuf.at[pl.ds(0, count)]
        return pltpu.make_async_copy(some, some, sem)

    rest = pl.ds(1, GROUP - 1)
    hand = remote(xbuf.at[rest], xbuf.at[rest], f_sem.at[0], f_sem.at[1], 1)
    local[0].wait()

    @pl.when(me == 0)
    def _():
        hand.wait_recv()

    @pl.when(me != 0)
    def _():
        blocks(GROUP - 2, xr_sem.at[0]).wait()

    @pl.when(me == 1)
    def _():
        blocks(1, xr_sem.at[1]).wait()
        hand.start()

    local[1].wait()
    squares = jnp.zeros((2 * ROWS, HD), f32)

    def scaled(j, squares):
        x = jnp.concatenate(
            [xbuf[i, s].astype(f32) for i in (j, TP + j) for s in range(STEPS)], axis=0
        )
        for c in range(BLK // HD):
            piece = x[:, c * HD : (c + 1) * HD]
            squares = squares + piece * piece
        xw[:, j * BLK : (j + 1) * BLK] = (x * gainv[j]).astype(bf16)
        return squares

    for j in range(1, TP):
        squares = scaled(j, squares)
    for copy in weights:
        copy.wait()
    tail = xw[:, BLK:]
    acc_q = jnp.dot(tail, wqv[pl.ds(BLK, D - BLK), :], preferred_element_type=f32)
    acc_k = jnp.dot(tail, wkv[pl.ds(BLK, D - BLK), :], preferred_element_type=f32)
    acc_v = jnp.dot(tail, wvv[pl.ds(BLK, D - BLK), :], preferred_element_type=f32)

    @pl.when(me > 1)
    def _():
        blocks(1, xr_sem.at[1]).wait()

    squares = scaled(0, squares)
    head = xw[:, :BLK]
    acc_q = acc_q + jnp.dot(head, wqv[pl.ds(0, BLK), :], preferred_element_type=f32)
    acc_k = acc_k + jnp.dot(head, wkv[pl.ds(0, BLK), :], preferred_element_type=f32)
    acc_v = acc_v + jnp.dot(head, wvv[pl.ds(0, BLK), :], preferred_element_type=f32)
    inverse = lax.rsqrt(jnp.sum(squares, axis=-1, keepdims=True) / D + EPS)

    def rotated(value):
        value = value * inverse
        return (value * cosine + pltpu.roll(value, HD // 2, 1) * sine).astype(bf16)

    q = jnp.concatenate([rotated(acc_q[:, :HD]), rotated(acc_q[:, HD:])], axis=0)
    kk[pl.ds(NEW, 2 * ROWS), :] = rotated(acc_k)
    vv[pl.ds(NEW, 2 * ROWS), :] = (acc_v * inverse).astype(bf16)
    for copy in caches:
        copy.wait()

    s = lax.dot_general(q, kk[...], (((1,), (1,)), ((), ())), preferred_element_type=f32)
    table = bias[...]
    s = s * (HD**-0.5) + jnp.concatenate([table, table], axis=0)
    m = jnp.max(s, axis=-1, keepdims=True)
    p = jnp.exp(s - m)
    l = jnp.sum(p, axis=-1, keepdims=True)
    o = jnp.dot(p.astype(bf16), vv[...], preferred_element_type=f32)
    mixed = m + jnp.log(l)
    o = o / l
    lane4 = lax.broadcasted_iota(jnp.int32, (4 * ROWS, HD), 1)
    high = mixed.astype(bf16).astype(f32)
    middle = (mixed - high).astype(bf16).astype(f32)
    low = mixed - high - middle
    terms = jnp.where(lane4 < HD // 4, high, jnp.where(lane4 < HD // 2, middle, low)).astype(bf16)
    rounded = o.astype(bf16)
    for half in range(2):
        for h in range(2):
            rows = slice((2 * h + half) * ROWS, (2 * h + half + 1) * ROWS)
            part[half, h * ROWS : (h + 1) * ROWS] = rounded[rows]
            part[half, (2 + h) * ROWS : (3 + h) * ROWS] = terms[rows]
    pcopy = remote(part.at[1 - parity], precv, p_sem.at[0], p_sem.at[1], TP)
    pcopy.start()
    for half in range(2):
        for h in range(2):
            rows = slice((2 * h + half) * ROWS, (2 * h + half + 1) * ROWS)
            kept[half, h * ROWS : (h + 1) * ROWS] = o[rows]
            kept[half, (2 + h) * ROWS : (3 + h) * ROWS] = jnp.broadcast_to(mixed, o.shape)[rows]
    outw[0].wait()

    @pl.when(me == 0)
    def _():
        blocks(GROUP - 1, xs_sem.at[0]).wait()

    @pl.when(me != 0)
    def _():
        blocks(GROUP - 2, xs_sem.at[0]).wait()

    @pl.when(me == 1)
    def _():
        hand.wait_send()

    mine = kept[parity]
    o1, m1 = mine[: 2 * ROWS], mine[2 * ROWS :]
    pcopy.wait_recv()
    other = precv[...].astype(f32)
    o2, terms = other[: 2 * ROWS], other[2 * ROWS :]
    m2 = terms[:, :1] + terms[:, HD // 4 : HD // 4 + 1] + terms[:, HD // 2 : HD // 2 + 1]
    top = jnp.maximum(m1, m2)
    e1 = jnp.exp(m1 - top)
    e2 = jnp.exp(m2 - top)
    context = ((o1 * e1 + o2 * e2) / (e1 + e2)).astype(bf16)
    context = jnp.concatenate([context[:ROWS], context[ROWS:]], axis=1)

    def outputs(ref, sem):
        some = ref.at[pl.ds(1, TP - 1)]
        return pltpu.make_async_copy(some, some, sem)

    product = jnp.dot(context, wov[...], preferred_element_type=f32).astype(bf16)
    for j in range(TP):
        osend[j] = product[:, j * BLK : (j + 1) * BLK]
    for k in FAR:
        remote(
            osend.at[member[k] % TP], orecv.at[k], os_sem.at[0], or_sem.at[0], k
        ).start()
    total = osend[tp].astype(f32)
    pcopy.wait_send()
    outputs(orecv, or_sem.at[0]).wait()
    for k in range(1, TP):
        total = total + orecv[k].astype(f32)
    total = total.astype(bf16)
    for s in range(STEPS):
        out[s] = total[s * OWN : (s + 1) * OWN]

    outputs(osend, os_sem.at[0]).wait()


def body(
    hidden_in, norm_gain, w_query, w_key, w_value, w_out,
    prompt_keys, prompt_values, gen_keys, gen_values, lengths, parents,
):
    operands = [
        hidden_in,
        norm_gain.reshape(TP, 1, BLK),
        w_query,
        w_key,
        w_value,
        w_out,
        prompt_keys.reshape(HALF, HD),
        prompt_values.reshape(HALF, HD),
        gen_keys,
        gen_values,
        lengths,
        parents,
    ]
    dma = pltpu.SemaphoreType.DMA
    anywhere = pl.BlockSpec(memory_space=pltpu.HBM)
    return pl.pallas_call(
        kernel,
        out_shape=jax.ShapeDtypeStruct((STEPS, OWN, BLK), bf16),
        in_specs=[anywhere] * 12,
        out_specs=pl.BlockSpec(memory_space=pltpu.VMEM),
        scratch_shapes=[
            pltpu.VMEM((GROUP, STEPS, OWN, BLK), bf16),
            pltpu.VMEM((2 * ROWS, D), bf16),
            pltpu.VMEM((TP, 1, BLK), f32),
            pltpu.VMEM((D, 2 * HD), bf16),
            pltpu.VMEM((D, HD), bf16),
            pltpu.VMEM((D, HD), bf16),
            pltpu.VMEM((2 * HD, D), bf16),
            pltpu.VMEM((KEYS, HD), bf16),
            pltpu.VMEM((KEYS, HD), bf16),
            pltpu.SMEM((32,), jnp.int32),
            pltpu.SMEM((STEPS, 256), jnp.int32),
            pltpu.VMEM((2 * ROWS, KEYS), f32),
            pltpu.VMEM((2, 4 * ROWS, HD), bf16),
            pltpu.VMEM((2, 4 * ROWS, HD), f32),
            pltpu.VMEM((4 * ROWS, HD), bf16),
            pltpu.VMEM((TP, ROWS, BLK), bf16),
            pltpu.VMEM((TP, ROWS, BLK), bf16),
            dma((6,)), dma((4,)), dma((TP,)), dma((OWN,)), dma((OWN,)),
            dma((1,)), dma((2,)), dma((2,)), dma((2,)), dma((1,)), dma((1,)),
        ],
        compiler_params=pltpu.CompilerParams(
            collective_id=0, has_side_effects=True, vmem_limit_bytes=24 * 2**20
        ),
        name="decode_block",
    )(*[pltpu.with_memory_space_constraint(x, pltpu.HBM) for x in operands])


def solution(mesh):
    in_specs = (
        P(None, "req", "tp"),
        P(),
        P(None, "tp"),
        P(None, "tp"),
        P(None, "tp"),
        P("tp", None),
        P("req", None, "tp"),
        P("req", None, "tp"),
        P("req", None, "tp"),
        P("req", None, "tp"),
        P(),
        P(),
    )
    out_specs = P(None, "req", "tp")
    return jax.shard_map(body, mesh=mesh, in_specs=in_specs, out_specs=out_specs, check_vma=False)
```

```python
import math

import jax
import jax.numpy as jnp
from jax import lax
from jax.experimental import pallas as pl
from jax.experimental.pallas import tpu as pltpu
from jax.sharding import PartitionSpec as P

HD = 128
TP = 8
STEPS = 4
OWN = 4
BEAMS = 8
ROWS = STEPS * OWN
BLK = 384
D = TP * BLK
HALF = 512
GEN = 64
KEYS = HALF + OWN * GEN + 128
NEW = HALF + OWN * GEN
EPS = 1e-05
NEG = -1e30
ROPE_BASE = 500000.0
GROUP = 2 * TP
FAR_GROUP = (12, 13, 4, 5, 1, 10, 11, 14, 15, 2, 3, 6, 7, 8, 9)
FAR = (4, 5, 2, 3, 6, 7, 1)

X_SENT, X_HERE, FIRST_HERE, LENGTHS, PARENTS, PART_HERE, OUT_HERE, WQ, WKV, CACHE, WO = range(11)
HANDED, PART_SENT, OUT_SENT = LENGTHS, PARENTS, X_SENT

bf16 = jnp.bfloat16
f32 = jnp.float32


def flip(index, k):
    result = 0
    for bit in (1, 2, 4, 8):
        digit = (index // bit) % 2
        result += bit * ((1 - digit) if k & bit else digit)
    return result


def kernel(
    hidden, gain, wq, wk, wv, wo, pk, pv, gk, gv, lengths, parents,
    out,
    xbuf, xw, gainv, wqv, wkv, wov, kv, lens, par, bias, part, kept, precv, osend, orecv, sem,
):
    req = lax.axis_index("req")
    tp = lax.axis_index("tp")
    parity = req % 2
    request = req // 2
    me = parity * TP + tp
    member = [flip(me, k) for k in range(GROUP)]

    def device(k):
        there = {}
        if k % TP:
            there["tp"] = member[k] % TP
        if k >= TP:
            there["req"] = req + 1 - 2 * parity
        return there

    def remote(src, dst, send, recv, k):
        return pltpu.make_async_remote_copy(
            src_ref=src, dst_ref=dst, send_sem=send, recv_sem=recv,
            device_id=device(k), device_id_type=pl.DeviceIdType.MESH,
        )

    barrier = pltpu.get_barrier_semaphore()

    @pl.when(me != 0)
    def _():
        for k in FAR_GROUP:
            pl.semaphore_signal(
                barrier, inc=1, device_id=device(k), device_id_type=pl.DeviceIdType.MESH
            )

    @pl.when(me == 0)
    def _():
        pl.semaphore_wait(barrier, GROUP - 1)

    @pl.when(me != 0)
    def _():
        pl.semaphore_wait(barrier, GROUP - 2)

    first = 1 - jnp.minimum(me, 1)
    xcopy = {}
    for k in FAR_GROUP:
        xcopy[k] = remote(hidden, xbuf.at[me], sem.at[X_SENT], sem.at[X_HERE + first], k)

        @pl.when(me != k)
        def _():
            xcopy[k].start()

    for source, target, which in (
        (hidden, xbuf.at[me], X_HERE),
        (gain, gainv, X_HERE),
        (lengths, lens, LENGTHS),
        (parents, par, PARENTS),
        (wq, wqv, WQ),
        (wk, wkv.at[0], WKV),
        (wv, wkv.at[1], WKV),
        (pk, kv.at[0, pl.ds(0, HALF)], CACHE),
        (pv, kv.at[1, pl.ds(0, HALF)], CACHE),
        (gk, kv.at[0, pl.ds(HALF, OWN * GEN)], CACHE),
        (gv, kv.at[1, pl.ds(HALF, OWN * GEN)], CACHE),
        (wo, wov, WO),
    ):
        pltpu.make_async_copy(source, target, sem.at[which]).start()

    def wait(ref, which):
        pltpu.make_async_copy(ref, ref, sem.at[which]).wait()

    wait(lens, LENGTHS)
    wait(par, PARENTS)
    length = lens[request]
    row = lax.broadcasted_iota(jnp.int32, (2 * ROWS, HD), 0)
    lane = lax.broadcasted_iota(jnp.int32, (2 * ROWS, HD), 1)
    position = (length + GEN + (row % ROWS) // OWN).astype(f32)
    frequency = jnp.exp((lane % (HD // 2)).astype(f32) * (-math.log(ROPE_BASE) / (HD // 2)))
    angle = position * frequency
    cosine = jnp.cos(angle)
    sine = jnp.sin(angle)
    sine = jnp.where(lane < HD // 2, -sine, sine)

    wide = lax.broadcasted_iota(jnp.int32, (2 * ROWS, HALF), 1)
    prompt_bias = jnp.where(parity * HALF + wide < length, 0.0, NEG).astype(f32)
    gen_beam = OWN * parity + lax.broadcasted_iota(jnp.int32, (2 * ROWS, OWN * GEN), 1) // GEN
    gen_from = jnp.zeros((2 * ROWS, HD), jnp.int32)
    new_from = jnp.full((2 * ROWS, HD), -1, jnp.int32)
    for half in range(2):
        for s in range(STEPS):
            for b in range(OWN):
                here = row == half * ROWS + s * OWN + b
                at = half * OWN + b
                for t in range(s, -1, -1):
                    new_from = jnp.where(here & ((lane % ROWS) // OWN == t), at, new_from)
                    at = par[t, request * BEAMS + at]
                gen_from = jnp.where(here, at, gen_from)
    gen_from = jnp.concatenate([gen_from, gen_from], axis=1)
    gen_bias = jnp.where(gen_from == gen_beam, 0.0, NEG).astype(f32)
    owned = lane // ROWS == parity
    new_bias = jnp.where(owned & (new_from == OWN * parity + lane % OWN), 0.0, NEG).astype(f32)
    bias[...] = jnp.concatenate([prompt_bias, gen_bias, new_bias], axis=1)
    zero = jnp.zeros((128, HD), bf16)
    kv[0, pl.ds(NEW, 128), :] = zero
    kv[1, pl.ds(NEW, 128), :] = zero

    rest = pl.ds(1, GROUP - 1)
    hand = remote(xbuf.at[rest], xbuf.at[rest], sem.at[HANDED], sem.at[FIRST_HERE], 1)

    @pl.when(me == 0)
    def _():
        wait(xbuf.at[pl.ds(0, 2)], X_HERE)
        hand.wait_recv()

    @pl.when(me != 0)
    def _():
        wait(xbuf, X_HERE)

    @pl.when(me == 1)
    def _():
        wait(xbuf.at[0], FIRST_HERE)
        hand.start()

    squares = jnp.zeros((2 * ROWS, HD), f32)

    def scaled(j, squares):
        x = jnp.concatenate(
            [xbuf[i, s].astype(f32) for i in (j, TP + j) for s in range(STEPS)], axis=0
        )
        for c in range(BLK // HD):
            piece = x[:, c * HD : (c + 1) * HD]
            squares = squares + piece * piece
        xw[:, j * BLK : (j + 1) * BLK] = (x * gainv[j]).astype(bf16)
        return squares

    for j in range(1, TP):
        squares = scaled(j, squares)
    wait(wqv, WQ)
    wait(wkv, WKV)
    tail = xw[:, BLK:]
    acc_q = jnp.dot(tail, wqv[pl.ds(BLK, D - BLK), :], preferred_element_type=f32)
    acc_k = jnp.dot(tail, wkv[0, pl.ds(BLK, D - BLK), :], preferred_element_type=f32)
    acc_v = jnp.dot(tail, wkv[1, pl.ds(BLK, D - BLK), :], preferred_element_type=f32)

    wait(kv.at[:, pl.ds(0, NEW)], CACHE)

    @pl.when(me > 1)
    def _():
        wait(xbuf.at[0], FIRST_HERE)

    squares = scaled(0, squares)
    head = xw[:, :BLK]
    acc_q = acc_q + jnp.dot(head, wqv[pl.ds(0, BLK), :], preferred_element_type=f32)
    acc_k = acc_k + jnp.dot(head, wkv[0, pl.ds(0, BLK), :], preferred_element_type=f32)
    acc_v = acc_v + jnp.dot(head, wkv[1, pl.ds(0, BLK), :], preferred_element_type=f32)
    inverse = lax.rsqrt(jnp.sum(squares, axis=-1, keepdims=True) / D + EPS)

    def rotated(value):
        value = value * inverse
        return (value * cosine + pltpu.roll(value, HD // 2, 1) * sine).astype(bf16)

    q = jnp.concatenate([rotated(acc_q[:, :HD]), rotated(acc_q[:, HD:])], axis=0)
    kv[0, pl.ds(NEW, 2 * ROWS), :] = rotated(acc_k)
    kv[1, pl.ds(NEW, 2 * ROWS), :] = (acc_v * inverse).astype(bf16)

    s = lax.dot_general(q, kv[0], (((1,), (1,)), ((), ())), preferred_element_type=f32)
    table = bias[...]
    s = s * (HD**-0.5) + jnp.concatenate([table, table], axis=0)
    m = jnp.max(s, axis=-1, keepdims=True)
    p = jnp.exp(s - m)
    l = jnp.sum(p, axis=-1, keepdims=True)
    o = jnp.dot(p.astype(bf16), kv[1], preferred_element_type=f32)
    mixed = m + jnp.log(l)
    o = o / l
    lane4 = lax.broadcasted_iota(jnp.int32, (4 * ROWS, HD), 1)
    high = mixed.astype(bf16).astype(f32)
    middle = (mixed - high).astype(bf16).astype(f32)
    low = mixed - high - middle
    terms = jnp.where(lane4 < HD // 4, high, jnp.where(lane4 < HD // 2, middle, low)).astype(bf16)
    rounded = o.astype(bf16)
    for half in range(2):
        for h in range(2):
            rows = slice((2 * h + half) * ROWS, (2 * h + half + 1) * ROWS)
            part[half, h * ROWS : (h + 1) * ROWS] = rounded[rows]
            part[half, (2 + h) * ROWS : (3 + h) * ROWS] = terms[rows]
    pcopy = remote(part.at[1 - parity], precv, sem.at[PART_SENT], sem.at[PART_HERE], TP)
    pcopy.start()
    for half in range(2):
        for h in range(2):
            rows = slice((2 * h + half) * ROWS, (2 * h + half + 1) * ROWS)
            kept[half, h * ROWS : (h + 1) * ROWS] = o[rows]
            kept[half, (2 + h) * ROWS : (3 + h) * ROWS] = jnp.broadcast_to(mixed, o.shape)[rows]
    wait(wov, WO)

    @pl.when(me == 0)
    def _():
        wait(xbuf.at[rest], X_SENT)

    @pl.when(me != 0)
    def _():
        wait(xbuf.at[pl.ds(0, GROUP - 2)], X_SENT)

    @pl.when(me == 1)
    def _():
        hand.wait_send()

    mine = kept[parity]
    o1, m1 = mine[: 2 * ROWS], mine[2 * ROWS :]
    pcopy.wait_recv()
    other = precv[...].astype(f32)
    o2, terms = other[: 2 * ROWS], other[2 * ROWS :]
    m2 = terms[:, :1] + terms[:, HD // 4 : HD // 4 + 1] + terms[:, HD // 2 : HD // 2 + 1]
    top = jnp.maximum(m1, m2)
    e1 = jnp.exp(m1 - top)
    e2 = jnp.exp(m2 - top)
    context = ((o1 * e1 + o2 * e2) / (e1 + e2)).astype(bf16)
    context = jnp.concatenate([context[:ROWS], context[ROWS:]], axis=1)

    product = jnp.dot(context, wov[...], preferred_element_type=f32).astype(bf16)
    for j in range(TP):
        osend[j] = product[:, j * BLK : (j + 1) * BLK]
    for k in FAR:
        remote(
            osend.at[member[k] % TP], orecv.at[k], sem.at[OUT_SENT], sem.at[OUT_HERE], k
        ).start()
    total = osend[tp].astype(f32)
    pcopy.wait_send()
    seven = pl.ds(1, TP - 1)
    wait(orecv.at[seven], OUT_HERE)
    for k in range(1, TP):
        total = total + orecv[k].astype(f32)
    total = total.astype(bf16)
    for s in range(STEPS):
        out[s] = total[s * OWN : (s + 1) * OWN]

    wait(osend.at[seven], OUT_SENT)


def body(
    hidden_in, norm_gain, w_query, w_key, w_value, w_out,
    prompt_keys, prompt_values, gen_keys, gen_values, lengths, parents,
):
    operands = [
        hidden_in,
        norm_gain.reshape(TP, 1, BLK),
        w_query,
        w_key,
        w_value,
        w_out,
        prompt_keys.reshape(HALF, HD),
        prompt_values.reshape(HALF, HD),
        gen_keys.reshape(OWN * GEN, HD),
        gen_values.reshape(OWN * GEN, HD),
        lengths,
        parents,
    ]
    anywhere = pl.BlockSpec(memory_space=pltpu.HBM)
    return pl.pallas_call(
        kernel,
        out_shape=jax.ShapeDtypeStruct((STEPS, OWN, BLK), bf16),
        in_specs=[anywhere] * 12,
        out_specs=pl.BlockSpec(memory_space=pltpu.VMEM),
        scratch_shapes=[
            pltpu.VMEM((GROUP, STEPS, OWN, BLK), bf16),
            pltpu.VMEM((2 * ROWS, D), bf16),
            pltpu.VMEM((TP, 1, BLK), f32),
            pltpu.VMEM((D, 2 * HD), bf16),
            pltpu.VMEM((2, D, HD), bf16),
            pltpu.VMEM((2 * HD, D), bf16),
            pltpu.VMEM((2, KEYS, HD), bf16),
            pltpu.SMEM((32,), jnp.int32),
            pltpu.SMEM((STEPS, 256), jnp.int32),
            pltpu.VMEM((2 * ROWS, KEYS), f32),
            pltpu.VMEM((2, 4 * ROWS, HD), bf16),
            pltpu.VMEM((2, 4 * ROWS, HD), f32),
            pltpu.VMEM((4 * ROWS, HD), bf16),
            pltpu.VMEM((TP, ROWS, BLK), bf16),
            pltpu.VMEM((TP, ROWS, BLK), bf16),
            pltpu.SemaphoreType.DMA((WO + 1,)),
        ],
        compiler_params=pltpu.CompilerParams(
            collective_id=0, has_side_effects=True, vmem_limit_bytes=24 * 2**20
        ),
        name="decode_block",
    )(*[pltpu.with_memory_space_constraint(x, pltpu.HBM) for x in operands])


def solution(mesh):
    in_specs = (
        P(None, "req", "tp"),
        P(),
        P(None, "tp"),
        P(None, "tp"),
        P(None, "tp"),
        P("tp", None),
        P("req", None, "tp"),
        P("req", None, "tp"),
        P("req", None, "tp"),
        P("req", None, "tp"),
        P(),
        P(),
    )
    out_specs = P(None, "req", "tp")
    return jax.shard_map(body, mesh=mesh, in_specs=in_specs, out_specs=out_specs, check_vma=False)
```

```python
import math

import jax
import jax.numpy as jnp
from jax import lax
from jax.experimental import pallas as pl
from jax.experimental.pallas import tpu as pltpu
from jax.sharding import PartitionSpec as P

HD = 128
TP = 8
STEPS = 4
OWN = 4
BEAMS = 8
ROWS = STEPS * OWN
BLK = 384
D = TP * BLK
HALF = 512
GEN = 64
KEYS = HALF + OWN * GEN + 128
NEW = HALF + OWN * GEN
EPS = 1e-05
NEG = -1e30
ROPE_BASE = 500000.0
GROUP = 2 * TP
FAR_GROUP = (12, 13, 4, 5, 1, 10, 11, 14, 15, 2, 3, 6, 7, 8, 9)
EARLY = 5
FAR = (4, 5, 2, 3, 6, 7, 1)

X_SENT, X_HERE, FIRST_HERE, LENGTHS, PARENTS, PART_HERE, OUT_HERE, WQ, WKV, CACHE, WO, FAR_HERE = (
    range(12)
)
HANDED, PART_SENT, OUT_SENT, FAR_SENT = LENGTHS, PARENTS, X_SENT, CACHE

bf16 = jnp.bfloat16
f32 = jnp.float32


def flip(index, k):
    result = 0
    for bit in (1, 2, 4, 8):
        digit = (index // bit) % 2
        result += bit * ((1 - digit) if k & bit else digit)
    return result


def kernel(
    hidden, gain, wq, wk, wv, wo, pk, pv, gk, gv, lengths, parents,
    out,
    xbuf, xw, gainv, wqv, wkv, wov, kv, lens, par, bias, part, kept, precv, osend, orecv, fsend, frecv, sem,
):
    req = lax.axis_index("req")
    tp = lax.axis_index("tp")
    parity = req % 2
    request = req // 2
    me = parity * TP + tp
    member = [flip(me, k) for k in range(GROUP)]

    def device(k):
        there = {}
        if k % TP:
            there["tp"] = member[k] % TP
        if k >= TP:
            there["req"] = req + 1 - 2 * parity
        return there

    def remote(src, dst, send, recv, k):
        return pltpu.make_async_remote_copy(
            src_ref=src, dst_ref=dst, send_sem=send, recv_sem=recv,
            device_id=device(k), device_id_type=pl.DeviceIdType.MESH,
        )

    barrier = pltpu.get_barrier_semaphore()

    @pl.when(me != 0)
    def _():
        for k in FAR_GROUP:
            pl.semaphore_signal(
                barrier, inc=1, device_id=device(k), device_id_type=pl.DeviceIdType.MESH
            )

    @pl.when(me == 0)
    def _():
        pl.semaphore_wait(barrier, GROUP - 1)

    @pl.when(me != 0)
    def _():
        pl.semaphore_wait(barrier, GROUP - 2)

    first = 1 - jnp.minimum(me, 1)
    xcopy = {}

    def send(k):
        xcopy[k] = remote(hidden, xbuf.at[me], sem.at[X_SENT], sem.at[X_HERE + first], k)

        @pl.when(me != k)
        def _():
            xcopy[k].start()

    for k in FAR_GROUP[:EARLY]:
        send(k)
    for source, target, which in (
        (hidden, xbuf.at[me], X_HERE),
        (gain, gainv, X_HERE),
        (lengths, lens, LENGTHS),
        (parents, par, PARENTS),
        (wq, wqv, WQ),
        (wk, wkv.at[0], WKV),
        (wv, wkv.at[1], WKV),
        (pk, kv.at[0, pl.ds(0, HALF)], CACHE),
        (pv, kv.at[1, pl.ds(0, HALF)], CACHE),
        (gk, kv.at[0, pl.ds(HALF, OWN * GEN)], CACHE),
        (gv, kv.at[1, pl.ds(HALF, OWN * GEN)], CACHE),
        (wo, wov, WO),
    ):
        pltpu.make_async_copy(source, target, sem.at[which]).start()

    for k in FAR_GROUP[EARLY:]:
        send(k)

    def wait(ref, which):
        pltpu.make_async_copy(ref, ref, sem.at[which]).wait()

    wait(lens, LENGTHS)
    wait(par, PARENTS)
    length = lens[request]
    row = lax.broadcasted_iota(jnp.int32, (2 * ROWS, HD), 0)
    lane = lax.broadcasted_iota(jnp.int32, (2 * ROWS, HD), 1)
    position = (length + GEN + (row % ROWS) // OWN).astype(f32)
    frequency = jnp.exp((lane % (HD // 2)).astype(f32) * (-math.log(ROPE_BASE) / (HD // 2)))
    angle = position * frequency
    cosine = jnp.cos(angle)
    sine = jnp.sin(angle)
    sine = jnp.where(lane < HD // 2, -sine, sine)

    wide = lax.broadcasted_iota(jnp.int32, (2 * ROWS, HALF), 1)
    prompt_bias = jnp.where(parity * HALF + wide < length, 0.0, NEG).astype(f32)
    gen_beam = OWN * parity + lax.broadcasted_iota(jnp.int32, (2 * ROWS, OWN * GEN), 1) // GEN
    gen_from = jnp.zeros((2 * ROWS, HD), jnp.int32)
    new_from = jnp.full((2 * ROWS, HD), -1, jnp.int32)
    for half in range(2):
        for s in range(STEPS):
            for b in range(OWN):
                here = row == half * ROWS + s * OWN + b
                at = half * OWN + b
                for t in range(s, -1, -1):
                    new_from = jnp.where(here & ((lane % ROWS) // OWN == t), at, new_from)
                    at = par[t, request * BEAMS + at]
                gen_from = jnp.where(here, at, gen_from)
    gen_from = jnp.concatenate([gen_from, gen_from], axis=1)
    gen_bias = jnp.where(gen_from == gen_beam, 0.0, NEG).astype(f32)
    owned = lane // ROWS == parity
    new_bias = jnp.where(owned & (new_from == OWN * parity + lane % OWN), 0.0, NEG).astype(f32)
    bias[...] = jnp.concatenate([prompt_bias, gen_bias, new_bias], axis=1)
    zero = jnp.zeros((128, HD), bf16)
    kv[0, pl.ds(NEW, 128), :] = zero
    kv[1, pl.ds(NEW, 128), :] = zero

    rest = pl.ds(1, GROUP - 1)
    hand = remote(xbuf.at[rest], xbuf.at[rest], sem.at[HANDED], sem.at[FIRST_HERE], 1)

    @pl.when(me == 0)
    def _():
        wait(xbuf.at[pl.ds(0, 2)], X_HERE)
        hand.wait_recv()

    @pl.when(me != 0)
    def _():
        wait(xbuf, X_HERE)

    @pl.when(me == 1)
    def _():
        wait(xbuf.at[0], FIRST_HERE)
        hand.start()

    squares = jnp.zeros((2 * ROWS, HD), f32)

    def scaled(j, squares):
        x = jnp.concatenate(
            [xbuf[i, s].astype(f32) for i in (j, TP + j) for s in range(STEPS)], axis=0
        )
        for c in range(BLK // HD):
            piece = x[:, c * HD : (c + 1) * HD]
            squares = squares + piece * piece
        xw[:, j * BLK : (j + 1) * BLK] = (x * gainv[j]).astype(bf16)
        return squares

    for j in range(1, TP):
        squares = scaled(j, squares)
    wait(wqv, WQ)
    wait(wkv, WKV)
    tail = xw[:, BLK:]
    acc_q = jnp.dot(tail, wqv[pl.ds(BLK, D - BLK), :], preferred_element_type=f32)
    acc_k = jnp.dot(tail, wkv[0, pl.ds(BLK, D - BLK), :], preferred_element_type=f32)
    acc_v = jnp.dot(tail, wkv[1, pl.ds(BLK, D - BLK), :], preferred_element_type=f32)

    wait(kv.at[:, pl.ds(0, NEW)], CACHE)

    @pl.when(me > 1)
    def _():
        wait(xbuf.at[0], FIRST_HERE)

    squares = scaled(0, squares)
    head = xw[:, :BLK]
    acc_q = acc_q + jnp.dot(head, wqv[pl.ds(0, BLK), :], preferred_element_type=f32)
    acc_k = acc_k + jnp.dot(head, wkv[0, pl.ds(0, BLK), :], preferred_element_type=f32)
    acc_v = acc_v + jnp.dot(head, wkv[1, pl.ds(0, BLK), :], preferred_element_type=f32)
    inverse = lax.rsqrt(jnp.sum(squares, axis=-1, keepdims=True) / D + EPS)

    def rotated(value):
        value = value * inverse
        return (value * cosine + pltpu.roll(value, HD // 2, 1) * sine).astype(bf16)

    q = jnp.concatenate([rotated(acc_q[:, :HD]), rotated(acc_q[:, HD:])], axis=0)
    kv[0, pl.ds(NEW, 2 * ROWS), :] = rotated(acc_k)
    kv[1, pl.ds(NEW, 2 * ROWS), :] = (acc_v * inverse).astype(bf16)

    s = lax.dot_general(q, kv[0], (((1,), (1,)), ((), ())), preferred_element_type=f32)
    table = bias[...]
    s = s * (HD**-0.5) + jnp.concatenate([table, table], axis=0)
    m = jnp.max(s, axis=-1, keepdims=True)
    p = jnp.exp(s - m)
    l = jnp.sum(p, axis=-1, keepdims=True)
    o = jnp.dot(p.astype(bf16), kv[1], preferred_element_type=f32)
    mixed = m + jnp.log(l)
    o = o / l
    lane4 = lax.broadcasted_iota(jnp.int32, (4 * ROWS, HD), 1)
    high = mixed.astype(bf16).astype(f32)
    middle = (mixed - high).astype(bf16).astype(f32)
    low = mixed - high - middle
    terms = jnp.where(lane4 < HD // 4, high, jnp.where(lane4 < HD // 2, middle, low)).astype(bf16)
    rounded = o.astype(bf16)
    for half in range(2):
        for h in range(2):
            rows = slice((2 * h + half) * ROWS, (2 * h + half + 1) * ROWS)
            part[half, h * ROWS : (h + 1) * ROWS] = rounded[rows]
            part[half, (2 + h) * ROWS : (3 + h) * ROWS] = terms[rows]
    pcopy = remote(part.at[1 - parity], precv, sem.at[PART_SENT], sem.at[PART_HERE], TP)
    pcopy.start()
    for half in range(2):
        for h in range(2):
            rows = slice((2 * h + half) * ROWS, (2 * h + half + 1) * ROWS)
            kept[half, h * ROWS : (h + 1) * ROWS] = o[rows]
            kept[half, (2 + h) * ROWS : (3 + h) * ROWS] = jnp.broadcast_to(mixed, o.shape)[rows]
    wait(wov, WO)

    away = tp >= 2
    fcopy = pltpu.make_async_remote_copy(
        src_ref=fsend, dst_ref=frecv.at[parity, jnp.maximum(tp - 2, 0)],
        send_sem=sem.at[FAR_SENT], recv_sem=sem.at[FAR_HERE],
        device_id={"req": req - parity, "tp": tp * 0 + 1}, device_id_type=pl.DeviceIdType.MESH,
    )

    @pl.when(away)
    def _():
        for h in range(2):
            rows = slice(2 * h * ROWS, (2 * h + 1) * ROWS)
            columns = slice(h * HD, (h + 1) * HD)
            fsend[h] = jnp.dot(
                rounded[rows], wov[columns, BLK : 2 * BLK], preferred_element_type=f32
            ).astype(bf16)
            fsend[2, :, columns] = terms[rows]
        fsend[2, :, 2 * HD :] = jnp.zeros((ROWS, BLK - 2 * HD), bf16)
        fcopy.start()

    @pl.when(me == 0)
    def _():
        wait(xbuf.at[rest], X_SENT)

    @pl.when(me != 0)
    def _():
        wait(xbuf.at[pl.ds(0, GROUP - 2)], X_SENT)

    @pl.when(me == 1)
    def _():
        hand.wait_send()

    def summed(terms):
        return terms[:, :1] + terms[:, HD // 4 : HD // 4 + 1] + terms[:, HD // 2 : HD // 2 + 1]

    mine = kept[parity]
    o1, m1 = mine[: 2 * ROWS], mine[2 * ROWS :]
    pcopy.wait_recv()
    other = precv[...].astype(f32)
    o2, m2 = other[: 2 * ROWS], summed(other[2 * ROWS :])
    top = jnp.maximum(m1, m2)
    e1 = jnp.exp(m1 - top)
    e2 = jnp.exp(m2 - top)
    context = ((o1 * e1 + o2 * e2) / (e1 + e2)).astype(bf16)
    context = jnp.concatenate([context[:ROWS], context[ROWS:]], axis=1)

    product = jnp.dot(context, wov[...], preferred_element_type=f32).astype(bf16)
    for j in range(TP):
        osend[j] = product[:, j * BLK : (j + 1) * BLK]
    for k in FAR:
        ocopy = remote(
            osend.at[member[k] % TP], orecv.at[k], sem.at[OUT_SENT], sem.at[OUT_HERE], k
        )

        @pl.when(me != k ^ 1 if k != 1 else me >= 0)
        def _():
            ocopy.start()

    pcopy.wait_send()

    def finish(total):
        total = total.astype(bf16)
        for s in range(STEPS):
            out[s] = total[s * OWN : (s + 1) * OWN]

    @pl.when(me != 1)
    def _():
        total = osend[tp].astype(f32)
        wait(orecv.at[pl.ds(1, TP - 1)], OUT_HERE)
        for k in range(1, TP):
            total = total + orecv[k].astype(f32)
        finish(total)

    @pl.when(me == 1)
    def _():
        total = osend[tp].astype(f32)
        wait(frecv, FAR_HERE)
        for c in range(TP - 2):
            for h in range(2):
                columns = slice(h * HD, (h + 1) * HD)
                n1 = summed(frecv[0, c, 2, :, columns].astype(f32))
                n2 = summed(frecv[1, c, 2, :, columns].astype(f32))
                above = jnp.maximum(n1, n2)
                g1 = jnp.exp(n1 - above)
                g2 = jnp.exp(n2 - above)
                over = 1.0 / (g1 + g2)
                total = total + frecv[0, c, h].astype(f32) * (g1 * over)
                total = total + frecv[1, c, h].astype(f32) * (g2 * over)
        wait(orecv.at[pl.ds(1, 1)], OUT_HERE)
        total = total + orecv[1].astype(f32)
        finish(total)

    relieved = away & (parity == 0)

    @pl.when(relieved)
    def _():
        wait(osend.at[pl.ds(0, TP - 2)], OUT_SENT)

    @pl.when(jnp.logical_not(relieved))
    def _():
        wait(osend.at[pl.ds(0, TP - 1)], OUT_SENT)

    @pl.when(away)
    def _():
        fcopy.wait_send()


def body(
    hidden_in, norm_gain, w_query, w_key, w_value, w_out,
    prompt_keys, prompt_values, gen_keys, gen_values, lengths, parents,
):
    operands = [
        hidden_in,
        norm_gain.reshape(TP, 1, BLK),
        w_query,
        w_key,
        w_value,
        w_out,
        prompt_keys.reshape(HALF, HD),
        prompt_values.reshape(HALF, HD),
        gen_keys.reshape(OWN * GEN, HD),
        gen_values.reshape(OWN * GEN, HD),
        lengths,
        parents,
    ]
    anywhere = pl.BlockSpec(memory_space=pltpu.HBM)
    return pl.pallas_call(
        kernel,
        out_shape=jax.ShapeDtypeStruct((STEPS, OWN, BLK), bf16),
        in_specs=[anywhere] * 12,
        out_specs=pl.BlockSpec(memory_space=pltpu.VMEM),
        scratch_shapes=[
            pltpu.VMEM((GROUP, STEPS, OWN, BLK), bf16),
            pltpu.VMEM((2 * ROWS, D), bf16),
            pltpu.VMEM((TP, 1, BLK), f32),
            pltpu.VMEM((D, 2 * HD), bf16),
            pltpu.VMEM((2, D, HD), bf16),
            pltpu.VMEM((2 * HD, D), bf16),
            pltpu.VMEM((2, KEYS, HD), bf16),
            pltpu.SMEM((32,), jnp.int32),
            pltpu.SMEM((STEPS, 256), jnp.int32),
            pltpu.VMEM((2 * ROWS, KEYS), f32),
            pltpu.VMEM((2, 4 * ROWS, HD), bf16),
            pltpu.VMEM((2, 4 * ROWS, HD), f32),
            pltpu.VMEM((4 * ROWS, HD), bf16),
            pltpu.VMEM((TP, ROWS, BLK), bf16),
            pltpu.VMEM((TP, ROWS, BLK), bf16),
            pltpu.VMEM((3, ROWS, BLK), bf16),
            pltpu.VMEM((2, TP - 2, 3, ROWS, BLK), bf16),
            pltpu.SemaphoreType.DMA((FAR_HERE + 1,)),
        ],
        compiler_params=pltpu.CompilerParams(
            collective_id=0, has_side_effects=True, vmem_limit_bytes=24 * 2**20
        ),
        name="decode_block",
    )(*[pltpu.with_memory_space_constraint(x, pltpu.HBM) for x in operands])


def solution(mesh):
    in_specs = (
        P(None, "req", "tp"),
        P(),
        P(None, "tp"),
        P(None, "tp"),
        P(None, "tp"),
        P("tp", None),
        P("req", None, "tp"),
        P("req", None, "tp"),
        P("req", None, "tp"),
        P("req", None, "tp"),
        P(),
        P(),
    )
    out_specs = P(None, "req", "tp")
    return jax.shard_map(body, mesh=mesh, in_specs=in_specs, out_specs=out_specs, check_vma=False)
```

```python
import math

import jax
import jax.numpy as jnp
from jax import lax
from jax.experimental import pallas as pl
from jax.experimental.pallas import tpu as pltpu
from jax.sharding import PartitionSpec as P

HD = 128
TP = 8
STEPS = 4
OWN = 4
BEAMS = 8
ROWS = STEPS * OWN
BLK = 384
D = TP * BLK
HALF = 512
GEN = 64
KEYS = HALF + OWN * GEN + 128
NEW = HALF + OWN * GEN
EPS = 1e-05
NEG = -1e30
ROPE_BASE = 500000.0
GROUP = 2 * TP
FAR_GROUP = (12, 13, 4, 5, 1, 10, 11, 14, 15, 2, 3, 6, 7, 8, 9)
EARLY = 5
FAR = (4, 5, 2, 3, 6, 7, 1)

X_SENT, X_HERE, FIRST_HERE, LENGTHS, PARENTS, PART_HERE, OUT_HERE, WQ, WKV, CACHE, WO, FAR_HERE = (
    range(12)
)
HANDED, PART_SENT, OUT_SENT, FAR_SENT = LENGTHS, PARENTS, X_SENT, CACHE

bf16 = jnp.bfloat16
f32 = jnp.float32


def flip(index, k):
    result = 0
    for bit in (1, 2, 4, 8):
        digit = (index // bit) % 2
        result += bit * ((1 - digit) if k & bit else digit)
    return result


def kernel(
    hidden, gain, wq, wk, wv, wo, pk, pv, gk, gv, lengths, parents,
    out,
    xbuf, xw, gainv, wqv, wkv, wov, kv, lens, par, bias, part, kept, precv, osend, orecv, fsend, frecv, sem,
):
    req = lax.axis_index("req")
    tp = lax.axis_index("tp")
    parity = req % 2
    request = req // 2
    me = parity * TP + tp
    member = [flip(me, k) for k in range(GROUP)]

    def device(k):
        there = {}
        if k % TP:
            there["tp"] = member[k] % TP
        if k >= TP:
            there["req"] = req + 1 - 2 * parity
        return there

    def remote(src, dst, send, recv, k):
        return pltpu.make_async_remote_copy(
            src_ref=src, dst_ref=dst, send_sem=send, recv_sem=recv,
            device_id=device(k), device_id_type=pl.DeviceIdType.MESH,
        )

    barrier = pltpu.get_barrier_semaphore()

    @pl.when(me != 0)
    def _():
        for k in FAR_GROUP:
            pl.semaphore_signal(
                barrier, inc=1, device_id=device(k), device_id_type=pl.DeviceIdType.MESH
            )

    @pl.when(me == 0)
    def _():
        pl.semaphore_wait(barrier, GROUP - 1)

    @pl.when(me != 0)
    def _():
        pl.semaphore_wait(barrier, GROUP - 2)

    first = 1 - jnp.minimum(me, 1)
    xcopy = {}

    def send(k):
        xcopy[k] = remote(hidden, xbuf.at[me], sem.at[X_SENT], sem.at[X_HERE + first], k)

        @pl.when(me != k)
        def _():
            xcopy[k].start()

    for k in FAR_GROUP[:EARLY]:
        send(k)
    for source, target, which in (
        (hidden, xbuf.at[me], X_HERE),
        (gain, gainv, X_HERE),
        (lengths, lens, LENGTHS),
        (parents, par, PARENTS),
        (wq, wqv, WQ),
        (wk, wkv.at[0], WKV),
        (wv, wkv.at[1], WKV),
        (pk, kv.at[0, pl.ds(0, HALF)], CACHE),
        (pv, kv.at[1, pl.ds(0, HALF)], CACHE),
        (gk, kv.at[0, pl.ds(HALF, OWN * GEN)], CACHE),
        (gv, kv.at[1, pl.ds(HALF, OWN * GEN)], CACHE),
        (wo, wov, WO),
    ):
        pltpu.make_async_copy(source, target, sem.at[which]).start()

    for k in FAR_GROUP[EARLY:]:
        send(k)

    def wait(ref, which):
        pltpu.make_async_copy(ref, ref, sem.at[which]).wait()

    wait(lens, LENGTHS)
    wait(par, PARENTS)
    length = lens[request]
    row = lax.broadcasted_iota(jnp.int32, (2 * ROWS, HD), 0)
    lane = lax.broadcasted_iota(jnp.int32, (2 * ROWS, HD), 1)
    position = (length + GEN + (row % ROWS) // OWN).astype(f32)
    frequency = jnp.exp((lane % (HD // 2)).astype(f32) * (-math.log(ROPE_BASE) / (HD // 2)))
    angle = position * frequency
    cosine = jnp.cos(angle)
    sine = jnp.sin(angle)
    sine = jnp.where(lane < HD // 2, -sine, sine)

    wide = lax.broadcasted_iota(jnp.int32, (2 * ROWS, HALF), 1)
    prompt_bias = jnp.where(parity * HALF + wide < length, 0.0, NEG).astype(f32)
    gen_beam = OWN * parity + lax.broadcasted_iota(jnp.int32, (2 * ROWS, OWN * GEN), 1) // GEN
    gen_from = jnp.zeros((2 * ROWS, HD), jnp.int32)
    new_from = jnp.full((2 * ROWS, HD), -1, jnp.int32)
    for half in range(2):
        for s in range(STEPS):
            for b in range(OWN):
                here = row == half * ROWS + s * OWN + b
                at = half * OWN + b
                for t in range(s, -1, -1):
                    new_from = jnp.where(here & ((lane % ROWS) // OWN == t), at, new_from)
                    at = par[t, request * BEAMS + at]
                gen_from = jnp.where(here, at, gen_from)
    gen_from = jnp.concatenate([gen_from, gen_from], axis=1)
    gen_bias = jnp.where(gen_from == gen_beam, 0.0, NEG).astype(f32)
    owned = lane // ROWS == parity
    new_bias = jnp.where(owned & (new_from == OWN * parity + lane % OWN), 0.0, NEG).astype(f32)
    bias[...] = jnp.concatenate([prompt_bias, gen_bias, new_bias], axis=1)
    zero = jnp.zeros((128, HD), bf16)
    kv[0, pl.ds(NEW, 128), :] = zero
    kv[1, pl.ds(NEW, 128), :] = zero

    rest = pl.ds(1, GROUP - 1)
    hand = remote(xbuf.at[rest], xbuf.at[rest], sem.at[HANDED], sem.at[FIRST_HERE], 1)

    @pl.when(me == 0)
    def _():
        wait(xbuf.at[pl.ds(0, 2)], X_HERE)
        hand.wait_recv()

    @pl.when(me != 0)
    def _():
        wait(xbuf, X_HERE)

    @pl.when(me == 1)
    def _():
        wait(xbuf.at[0], FIRST_HERE)
        hand.start()

    squares = jnp.zeros((2 * ROWS, HD), f32)

    def scaled(j, squares):
        x = jnp.concatenate(
            [xbuf[i, s].astype(f32) for i in (j, TP + j) for s in range(STEPS)], axis=0
        )
        for c in range(BLK // HD):
            piece = x[:, c * HD : (c + 1) * HD]
            squares = squares + piece * piece
        xw[:, j * BLK : (j + 1) * BLK] = (x * gainv[j]).astype(bf16)
        return squares

    for j in range(1, TP):
        squares = scaled(j, squares)
    wait(wqv, WQ)
    wait(wkv, WKV)
    tail = xw[:, BLK:]
    acc_q = jnp.dot(tail, wqv[pl.ds(BLK, D - BLK), :], preferred_element_type=f32)
    acc_k = jnp.dot(tail, wkv[0, pl.ds(BLK, D - BLK), :], preferred_element_type=f32)
    acc_v = jnp.dot(tail, wkv[1, pl.ds(BLK, D - BLK), :], preferred_element_type=f32)

    wait(kv.at[:, pl.ds(0, NEW)], CACHE)

    @pl.when(me > 1)
    def _():
        wait(xbuf.at[0], FIRST_HERE)

    squares = scaled(0, squares)
    head = xw[:, :BLK]
    acc_q = acc_q + jnp.dot(head, wqv[pl.ds(0, BLK), :], preferred_element_type=f32)
    acc_k = acc_k + jnp.dot(head, wkv[0, pl.ds(0, BLK), :], preferred_element_type=f32)
    acc_v = acc_v + jnp.dot(head, wkv[1, pl.ds(0, BLK), :], preferred_element_type=f32)
    inverse = lax.rsqrt(jnp.sum(squares, axis=-1, keepdims=True) / D + EPS)

    def rotated(value):
        value = value * inverse
        return (value * cosine + pltpu.roll(value, HD // 2, 1) * sine).astype(bf16)

    q = jnp.concatenate([rotated(acc_q[:, :HD]), rotated(acc_q[:, HD:])], axis=0)
    kv[0, pl.ds(NEW, 2 * ROWS), :] = rotated(acc_k)
    kv[1, pl.ds(NEW, 2 * ROWS), :] = (acc_v * inverse).astype(bf16)

    s = lax.dot_general(q, kv[0], (((1,), (1,)), ((), ())), preferred_element_type=f32)
    table = bias[...]
    s = s * (HD**-0.5) + jnp.concatenate([table, table], axis=0)
    m = jnp.max(s, axis=-1, keepdims=True)
    p = jnp.exp(s - m)
    l = jnp.sum(p, axis=-1, keepdims=True)
    o = jnp.dot(p.astype(bf16), kv[1], preferred_element_type=f32)
    mixed = m + jnp.log(l)
    o = o / l
    lane4 = lax.broadcasted_iota(jnp.int32, (4 * ROWS, HD), 1)
    high = mixed.astype(bf16).astype(f32)
    middle = (mixed - high).astype(bf16).astype(f32)
    low = mixed - high - middle
    terms = jnp.where(lane4 < HD // 4, high, jnp.where(lane4 < HD // 2, middle, low)).astype(bf16)
    rounded = o.astype(bf16)
    for half in range(2):
        for h in range(2):
            rows = slice((2 * h + half) * ROWS, (2 * h + half + 1) * ROWS)
            part[half, h * ROWS : (h + 1) * ROWS] = rounded[rows]
            part[half, (2 + h) * ROWS : (3 + h) * ROWS] = terms[rows]
    pcopy = remote(part.at[1 - parity], precv, sem.at[PART_SENT], sem.at[PART_HERE], TP)
    pcopy.start()
    for half in range(2):
        for h in range(2):
            rows = slice((2 * h + half) * ROWS, (2 * h + half + 1) * ROWS)
            kept[half, h * ROWS : (h + 1) * ROWS] = o[rows]
            kept[half, (2 + h) * ROWS : (3 + h) * ROWS] = jnp.broadcast_to(mixed, o.shape)[rows]
    wait(wov, WO)

    away = tp >= 2
    fcopy = pltpu.make_async_remote_copy(
        src_ref=fsend, dst_ref=frecv.at[parity, jnp.maximum(tp - 2, 0)],
        send_sem=sem.at[FAR_SENT], recv_sem=sem.at[FAR_HERE],
        device_id={"req": req - parity, "tp": tp * 0 + 1}, device_id_type=pl.DeviceIdType.MESH,
    )

    @pl.when(away)
    def _():
        for h in range(2):
            rows = slice(2 * h * ROWS, (2 * h + 1) * ROWS)
            columns = slice(h * HD, (h + 1) * HD)
            fsend[:, h * BLK : (h + 1) * BLK] = jnp.dot(
                rounded[rows], wov[columns, BLK : 2 * BLK], preferred_element_type=f32
            ).astype(bf16)
        at = lax.broadcasted_iota(jnp.int32, (ROWS, HD), 1)
        packed = jnp.broadcast_to(low[2 * ROWS : 3 * ROWS], (ROWS, HD))
        for bound, value in (
            (96, middle[2 * ROWS : 3 * ROWS]),
            (80, high[2 * ROWS : 3 * ROWS]),
            (64, low[:ROWS]),
            (32, middle[:ROWS]),
            (16, high[:ROWS]),
        ):
            packed = jnp.where(at < bound, value, packed)
        fsend[:, 2 * BLK :] = packed.astype(bf16)
        fcopy.start()

    @pl.when(me == 0)
    def _():
        wait(xbuf.at[rest], X_SENT)

    @pl.when(me != 0)
    def _():
        wait(xbuf.at[pl.ds(0, GROUP - 2)], X_SENT)

    @pl.when(me == 1)
    def _():
        hand.wait_send()

    def summed(terms):
        return terms[:, :1] + terms[:, HD // 4 : HD // 4 + 1] + terms[:, HD // 2 : HD // 2 + 1]

    mine = kept[parity]
    o1, m1 = mine[: 2 * ROWS], mine[2 * ROWS :]
    pcopy.wait_recv()
    other = precv[...].astype(f32)
    o2, m2 = other[: 2 * ROWS], summed(other[2 * ROWS :])
    top = jnp.maximum(m1, m2)
    e1 = jnp.exp(m1 - top)
    e2 = jnp.exp(m2 - top)
    context = ((o1 * e1 + o2 * e2) / (e1 + e2)).astype(bf16)
    context = jnp.concatenate([context[:ROWS], context[ROWS:]], axis=1)

    product = jnp.dot(context, wov[...], preferred_element_type=f32).astype(bf16)
    for j in range(TP):
        osend[j] = product[:, j * BLK : (j + 1) * BLK]
    for k in FAR:
        ocopy = remote(
            osend.at[member[k] % TP], orecv.at[k], sem.at[OUT_SENT], sem.at[OUT_HERE], k
        )

        @pl.when(me != k ^ 1 if k != 1 else me >= 0)
        def _():
            ocopy.start()

    pcopy.wait_send()

    def finish(total):
        total = total.astype(bf16)
        for s in range(STEPS):
            out[s] = total[s * OWN : (s + 1) * OWN]

    @pl.when(me != 1)
    def _():
        total = osend[tp].astype(f32)
        wait(orecv.at[pl.ds(1, TP - 1)], OUT_HERE)
        for k in range(1, TP):
            total = total + orecv[k].astype(f32)
        finish(total)

    @pl.when(me == 1)
    def _():
        total = osend[tp].astype(f32)
        wait(frecv, FAR_HERE)
        for c in range(TP - 2):
            packed = [frecv[half, c, :, 2 * BLK :].astype(f32) for half in range(2)]
            for h in range(2):
                n1, n2 = (
                    t[:, 64 * h : 64 * h + 1]
                    + t[:, 64 * h + 16 : 64 * h + 17]
                    + t[:, 64 * h + 32 : 64 * h + 33]
                    for t in packed
                )
                above = jnp.maximum(n1, n2)
                g1 = jnp.exp(n1 - above)
                g2 = jnp.exp(n2 - above)
                over = 1.0 / (g1 + g2)
                columns = slice(h * BLK, (h + 1) * BLK)
                total = total + frecv[0, c, :, columns].astype(f32) * (g1 * over)
                total = total + frecv[1, c, :, columns].astype(f32) * (g2 * over)
        wait(orecv.at[pl.ds(1, 1)], OUT_HERE)
        total = total + orecv[1].astype(f32)
        finish(total)

    relieved = away & (parity == 0)

    @pl.when(relieved)
    def _():
        wait(osend.at[pl.ds(0, TP - 2)], OUT_SENT)

    @pl.when(jnp.logical_not(relieved))
    def _():
        wait(osend.at[pl.ds(0, TP - 1)], OUT_SENT)

    @pl.when(away)
    def _():
        fcopy.wait_send()


def body(
    hidden_in, norm_gain, w_query, w_key, w_value, w_out,
    prompt_keys, prompt_values, gen_keys, gen_values, lengths, parents,
):
    operands = [
        hidden_in,
        norm_gain.reshape(TP, 1, BLK),
        w_query,
        w_key,
        w_value,
        w_out,
        prompt_keys.reshape(HALF, HD),
        prompt_values.reshape(HALF, HD),
        gen_keys.reshape(OWN * GEN, HD),
        gen_values.reshape(OWN * GEN, HD),
        lengths,
        parents,
    ]
    anywhere = pl.BlockSpec(memory_space=pltpu.HBM)
    return pl.pallas_call(
        kernel,
        out_shape=jax.ShapeDtypeStruct((STEPS, OWN, BLK), bf16),
        in_specs=[anywhere] * 12,
        out_specs=pl.BlockSpec(memory_space=pltpu.VMEM),
        scratch_shapes=[
            pltpu.VMEM((GROUP, STEPS, OWN, BLK), bf16),
            pltpu.VMEM((2 * ROWS, D), bf16),
            pltpu.VMEM((TP, 1, BLK), f32),
            pltpu.VMEM((D, 2 * HD), bf16),
            pltpu.VMEM((2, D, HD), bf16),
            pltpu.VMEM((2 * HD, D), bf16),
            pltpu.VMEM((2, KEYS, HD), bf16),
            pltpu.SMEM((32,), jnp.int32),
            pltpu.SMEM((STEPS, 256), jnp.int32),
            pltpu.VMEM((2 * ROWS, KEYS), f32),
            pltpu.VMEM((2, 4 * ROWS, HD), bf16),
            pltpu.VMEM((2, 4 * ROWS, HD), f32),
            pltpu.VMEM((4 * ROWS, HD), bf16),
            pltpu.VMEM((TP, ROWS, BLK), bf16),
            pltpu.VMEM((TP, ROWS, BLK), bf16),
            pltpu.VMEM((ROWS, 2 * BLK + HD), bf16),
            pltpu.VMEM((2, TP - 2, ROWS, 2 * BLK + HD), bf16),
            pltpu.SemaphoreType.DMA((FAR_HERE + 1,)),
        ],
        compiler_params=pltpu.CompilerParams(
            collective_id=0, has_side_effects=True, vmem_limit_bytes=24 * 2**20
        ),
        name="decode_block",
    )(*[pltpu.with_memory_space_constraint(x, pltpu.HBM) for x in operands])


def solution(mesh):
    in_specs = (
        P(None, "req", "tp"),
        P(),
        P(None, "tp"),
        P(None, "tp"),
        P(None, "tp"),
        P("tp", None),
        P("req", None, "tp"),
        P("req", None, "tp"),
        P("req", None, "tp"),
        P("req", None, "tp"),
        P(),
        P(),
    )
    out_specs = P(None, "req", "tp")
    return jax.shard_map(body, mesh=mesh, in_specs=in_specs, out_specs=out_specs, check_vma=False)
```

```python
import math

import jax
import jax.numpy as jnp
from jax import lax
from jax.experimental import pallas as pl
from jax.experimental.pallas import tpu as pltpu
from jax.sharding import PartitionSpec as P

HD = 128
TP = 8
STEPS = 4
OWN = 4
BEAMS = 8
ROWS = STEPS * OWN
BLK = 384
D = TP * BLK
HALF = 512
GEN = 64
KEYS = HALF + OWN * GEN + 128
NEW = HALF + OWN * GEN
EPS = 1e-05
NEG = -1e30
ROPE_BASE = 500000.0
GROUP = 2 * TP
FAR_GROUP = (12, 13, 4, 5, 1, 10, 11, 14, 15, 2, 3, 6, 7, 8, 9)
EARLY = 5
FAR = (4, 5, 2, 3, 6, 7, 1)

X_SENT, X_HERE, FIRST_HERE, LENGTHS, PARENTS, PART_HERE, OUT_HERE, WQ, WKV, CACHE, WO, FAR_HERE = (
    range(12)
)
HANDED, PART_SENT, OUT_SENT, FAR_SENT = LENGTHS, PARENTS, X_SENT, CACHE

bf16 = jnp.bfloat16
f32 = jnp.float32


def flip(index, k):
    result = 0
    for bit in (1, 2, 4, 8):
        digit = (index // bit) % 2
        result += bit * ((1 - digit) if k & bit else digit)
    return result


def kernel(
    hidden, gain, wq, wk, wv, wo, pk, pv, gk, gv, lengths, parents,
    out,
    xbuf, xw, gainv, wqv, wkv, wov, kv, lens, par, bias, part, kept, precv, osend, orecv, fsend, frecv, sem,
):
    req = lax.axis_index("req")
    tp = lax.axis_index("tp")
    parity = req % 2
    request = req // 2
    me = parity * TP + tp
    member = [flip(me, k) for k in range(GROUP)]

    def device(k):
        there = {}
        if k % TP:
            there["tp"] = member[k] % TP
        if k >= TP:
            there["req"] = req + 1 - 2 * parity
        return there

    def remote(src, dst, send, recv, k):
        return pltpu.make_async_remote_copy(
            src_ref=src, dst_ref=dst, send_sem=send, recv_sem=recv,
            device_id=device(k), device_id_type=pl.DeviceIdType.MESH,
        )

    barrier = pltpu.get_barrier_semaphore()

    @pl.when(me != 0)
    def _():
        for k in FAR_GROUP:
            pl.semaphore_signal(
                barrier, inc=1, device_id=device(k), device_id_type=pl.DeviceIdType.MESH
            )

    staged = pltpu.make_async_copy(hidden, xbuf.at[me], sem.at[WO])

    @pl.when(me != 0)
    def _():
        staged.start()
        staged.wait()

    @pl.when(me == 0)
    def _():
        pl.semaphore_wait(barrier, GROUP - 1)

    @pl.when(me != 0)
    def _():
        pl.semaphore_wait(barrier, GROUP - 2)

    first = 1 - jnp.minimum(me, 1)
    xcopy = {}

    def send(k):
        xcopy[k] = remote(hidden, xbuf.at[me], sem.at[X_SENT], sem.at[X_HERE + first], k)

        @pl.when(me == 0)
        def _():
            xcopy[k].start()

        @pl.when((me != k) & (me != 0))
        def _():
            remote(xbuf.at[me], xbuf.at[me], sem.at[X_SENT], sem.at[X_HERE + first], k).start()

    for k in FAR_GROUP[:EARLY]:
        send(k)
    for source, target, which in (
        (gain, gainv, X_HERE),
        (lengths, lens, LENGTHS),
        (parents, par, PARENTS),
        (wq, wqv, WQ),
        (wk, wkv.at[0], WKV),
        (wv, wkv.at[1], WKV),
        (pk, kv.at[0, pl.ds(0, HALF)], CACHE),
        (pv, kv.at[1, pl.ds(0, HALF)], CACHE),
        (gk, kv.at[0, pl.ds(HALF, OWN * GEN)], CACHE),
        (gv, kv.at[1, pl.ds(HALF, OWN * GEN)], CACHE),
        (wo, wov, WO),
    ):
        pltpu.make_async_copy(source, target, sem.at[which]).start()

    for k in FAR_GROUP[EARLY:]:
        send(k)

    def wait(ref, which):
        pltpu.make_async_copy(ref, ref, sem.at[which]).wait()

    wait(lens, LENGTHS)
    wait(par, PARENTS)
    length = lens[request]
    row = lax.broadcasted_iota(jnp.int32, (2 * ROWS, HD), 0)
    lane = lax.broadcasted_iota(jnp.int32, (2 * ROWS, HD), 1)
    position = (length + GEN + (row % ROWS) // OWN).astype(f32)
    frequency = jnp.exp((lane % (HD // 2)).astype(f32) * (-math.log(ROPE_BASE) / (HD // 2)))
    angle = position * frequency
    cosine = jnp.cos(angle)
    sine = jnp.sin(angle)
    sine = jnp.where(lane < HD // 2, -sine, sine)

    wide = lax.broadcasted_iota(jnp.int32, (2 * ROWS, HALF), 1)
    prompt_bias = jnp.where(parity * HALF + wide < length, 0.0, NEG).astype(f32)
    gen_beam = OWN * parity + lax.broadcasted_iota(jnp.int32, (2 * ROWS, OWN * GEN), 1) // GEN
    gen_from = jnp.zeros((2 * ROWS, HD), jnp.int32)
    new_from = jnp.full((2 * ROWS, HD), -1, jnp.int32)
    for half in range(2):
        for s in range(STEPS):
            for b in range(OWN):
                here = row == half * ROWS + s * OWN + b
                at = half * OWN + b
                for t in range(s, -1, -1):
                    new_from = jnp.where(here & ((lane % ROWS) // OWN == t), at, new_from)
                    at = par[t, request * BEAMS + at]
                gen_from = jnp.where(here, at, gen_from)
    gen_from = jnp.concatenate([gen_from, gen_from], axis=1)
    gen_bias = jnp.where(gen_from == gen_beam, 0.0, NEG).astype(f32)
    owned = lane // ROWS == parity
    new_bias = jnp.where(owned & (new_from == OWN * parity + lane % OWN), 0.0, NEG).astype(f32)
    bias[...] = jnp.concatenate([prompt_bias, gen_bias, new_bias], axis=1)
    zero = jnp.zeros((128, HD), bf16)
    kv[0, pl.ds(NEW, 128), :] = zero
    kv[1, pl.ds(NEW, 128), :] = zero

    rest = pl.ds(1, GROUP - 1)
    hand = remote(xbuf.at[rest], xbuf.at[rest], sem.at[HANDED], sem.at[FIRST_HERE], 1)

    @pl.when(me == 0)
    def _():
        own = pltpu.make_async_copy(hidden, xbuf.at[0], sem.at[X_HERE])
        own.start()
        wait(xbuf.at[pl.ds(0, 2)], X_HERE)
        hand.wait_recv()

    @pl.when(me != 0)
    def _():
        wait(xbuf.at[rest], X_HERE)

    @pl.when(me == 1)
    def _():
        wait(xbuf.at[0], FIRST_HERE)
        hand.start()

    squares = jnp.zeros((2 * ROWS, HD), f32)

    def scaled(j, squares):
        x = jnp.concatenate(
            [xbuf[i, s].astype(f32) for i in (j, TP + j) for s in range(STEPS)], axis=0
        )
        for c in range(BLK // HD):
            piece = x[:, c * HD : (c + 1) * HD]
            squares = squares + piece * piece
        xw[:, j * BLK : (j + 1) * BLK] = (x * gainv[j]).astype(bf16)
        return squares

    for j in range(1, TP):
        squares = scaled(j, squares)
    wait(wqv, WQ)
    wait(wkv, WKV)
    tail = xw[:, BLK:]
    acc_q = jnp.dot(tail, wqv[pl.ds(BLK, D - BLK), :], preferred_element_type=f32)
    acc_k = jnp.dot(tail, wkv[0, pl.ds(BLK, D - BLK), :], preferred_element_type=f32)
    acc_v = jnp.dot(tail, wkv[1, pl.ds(BLK, D - BLK), :], preferred_element_type=f32)

    wait(kv.at[:, pl.ds(0, NEW)], CACHE)

    @pl.when(me > 1)
    def _():
        wait(xbuf.at[0], FIRST_HERE)

    squares = scaled(0, squares)
    head = xw[:, :BLK]
    acc_q = acc_q + jnp.dot(head, wqv[pl.ds(0, BLK), :], preferred_element_type=f32)
    acc_k = acc_k + jnp.dot(head, wkv[0, pl.ds(0, BLK), :], preferred_element_type=f32)
    acc_v = acc_v + jnp.dot(head, wkv[1, pl.ds(0, BLK), :], preferred_element_type=f32)
    inverse = lax.rsqrt(jnp.sum(squares, axis=-1, keepdims=True) / D + EPS)

    def rotated(value):
        value = value * inverse
        return (value * cosine + pltpu.roll(value, HD // 2, 1) * sine).astype(bf16)

    q = jnp.concatenate([rotated(acc_q[:, :HD]), rotated(acc_q[:, HD:])], axis=0)
    kv[0, pl.ds(NEW, 2 * ROWS), :] = rotated(acc_k)
    kv[1, pl.ds(NEW, 2 * ROWS), :] = (acc_v * inverse).astype(bf16)

    s = lax.dot_general(q, kv[0], (((1,), (1,)), ((), ())), preferred_element_type=f32)
    table = bias[...]
    s = s * (HD**-0.5) + jnp.concatenate([table, table], axis=0)
    m = jnp.max(s, axis=-1, keepdims=True)
    p = jnp.exp(s - m)
    l = jnp.sum(p, axis=-1, keepdims=True)
    o = jnp.dot(p.astype(bf16), kv[1], preferred_element_type=f32)
    mixed = m + jnp.log(l)
    o = o / l
    lane4 = lax.broadcasted_iota(jnp.int32, (4 * ROWS, HD), 1)
    high = mixed.astype(bf16).astype(f32)
    middle = (mixed - high).astype(bf16).astype(f32)
    low = mixed - high - middle
    terms = jnp.where(lane4 < HD // 4, high, jnp.where(lane4 < HD // 2, middle, low)).astype(bf16)
    rounded = o.astype(bf16)
    for half in range(2):
        for h in range(2):
            rows = slice((2 * h + half) * ROWS, (2 * h + half + 1) * ROWS)
            part[half, h * ROWS : (h + 1) * ROWS] = rounded[rows]
            part[half, (2 + h) * ROWS : (3 + h) * ROWS] = terms[rows]
    pcopy = remote(part.at[1 - parity], precv, sem.at[PART_SENT], sem.at[PART_HERE], TP)
    pcopy.start()
    for half in range(2):
        for h in range(2):
            rows = slice((2 * h + half) * ROWS, (2 * h + half + 1) * ROWS)
            kept[half, h * ROWS : (h + 1) * ROWS] = o[rows]
            kept[half, (2 + h) * ROWS : (3 + h) * ROWS] = jnp.broadcast_to(mixed, o.shape)[rows]
    wait(wov, WO)

    away = tp >= 2
    fcopy = pltpu.make_async_remote_copy(
        src_ref=fsend, dst_ref=frecv.at[parity, jnp.maximum(tp - 2, 0)],
        send_sem=sem.at[FAR_SENT], recv_sem=sem.at[FAR_HERE],
        device_id={"req": req - parity, "tp": tp * 0 + 1}, device_id_type=pl.DeviceIdType.MESH,
    )

    @pl.when(away)
    def _():
        for h in range(2):
            rows = slice(2 * h * ROWS, (2 * h + 1) * ROWS)
            columns = slice(h * HD, (h + 1) * HD)
            fsend[:, h * BLK : (h + 1) * BLK] = jnp.dot(
                rounded[rows], wov[columns, BLK : 2 * BLK], preferred_element_type=f32
            ).astype(bf16)
        at = lax.broadcasted_iota(jnp.int32, (ROWS, HD), 1)
        packed = jnp.broadcast_to(low[2 * ROWS : 3 * ROWS], (ROWS, HD))
        for bound, value in (
            (96, middle[2 * ROWS : 3 * ROWS]),
            (80, high[2 * ROWS : 3 * ROWS]),
            (64, low[:ROWS]),
            (32, middle[:ROWS]),
            (16, high[:ROWS]),
        ):
            packed = jnp.where(at < bound, value, packed)
        fsend[:, 2 * BLK :] = packed.astype(bf16)
        fcopy.start()

    @pl.when(me == 0)
    def _():
        wait(xbuf.at[rest], X_SENT)

    @pl.when(me != 0)
    def _():
        wait(xbuf.at[pl.ds(0, GROUP - 2)], X_SENT)

    @pl.when(me == 1)
    def _():
        hand.wait_send()

    def summed(terms):
        return terms[:, :1] + terms[:, HD // 4 : HD // 4 + 1] + terms[:, HD // 2 : HD // 2 + 1]

    mine = kept[parity]
    o1, m1 = mine[: 2 * ROWS], mine[2 * ROWS :]
    pcopy.wait_recv()
    other = precv[...].astype(f32)
    o2, m2 = other[: 2 * ROWS], summed(other[2 * ROWS :])
    top = jnp.maximum(m1, m2)
    e1 = jnp.exp(m1 - top)
    e2 = jnp.exp(m2 - top)
    context = ((o1 * e1 + o2 * e2) / (e1 + e2)).astype(bf16)
    context = jnp.concatenate([context[:ROWS], context[ROWS:]], axis=1)

    product = jnp.dot(context, wov[...], preferred_element_type=f32).astype(bf16)
    for j in range(TP):
        osend[j] = product[:, j * BLK : (j + 1) * BLK]
    for k in FAR:
        ocopy = remote(
            osend.at[member[k] % TP], orecv.at[k], sem.at[OUT_SENT], sem.at[OUT_HERE], k
        )

        @pl.when(me != k ^ 1 if k != 1 else me >= 0)
        def _():
            ocopy.start()

    pcopy.wait_send()

    def finish(total):
        total = total.astype(bf16)
        for s in range(STEPS):
            out[s] = total[s * OWN : (s + 1) * OWN]

    @pl.when(me != 1)
    def _():
        total = osend[tp].astype(f32)
        wait(orecv.at[pl.ds(1, TP - 1)], OUT_HERE)
        for k in range(1, TP):
            total = total + orecv[k].astype(f32)
        finish(total)

    @pl.when(me == 1)
    def _():
        total = osend[tp].astype(f32)
        wait(frecv, FAR_HERE)
        for c in range(TP - 2):
            packed = [frecv[half, c, :, 2 * BLK :].astype(f32) for half in range(2)]
            for h in range(2):
                n1, n2 = (
                    t[:, 64 * h : 64 * h + 1]
                    + t[:, 64 * h + 16 : 64 * h + 17]
                    + t[:, 64 * h + 32 : 64 * h + 33]
                    for t in packed
                )
                above = jnp.maximum(n1, n2)
                g1 = jnp.exp(n1 - above)
                g2 = jnp.exp(n2 - above)
                over = 1.0 / (g1 + g2)
                columns = slice(h * BLK, (h + 1) * BLK)
                total = total + frecv[0, c, :, columns].astype(f32) * (g1 * over)
                total = total + frecv[1, c, :, columns].astype(f32) * (g2 * over)
        wait(orecv.at[pl.ds(1, 1)], OUT_HERE)
        total = total + orecv[1].astype(f32)
        finish(total)

    relieved = away & (parity == 0)

    @pl.when(relieved)
    def _():
        wait(osend.at[pl.ds(0, TP - 2)], OUT_SENT)

    @pl.when(jnp.logical_not(relieved))
    def _():
        wait(osend.at[pl.ds(0, TP - 1)], OUT_SENT)

    @pl.when(away)
    def _():
        fcopy.wait_send()


def body(
    hidden_in, norm_gain, w_query, w_key, w_value, w_out,
    prompt_keys, prompt_values, gen_keys, gen_values, lengths, parents,
):
    operands = [
        hidden_in,
        norm_gain.reshape(TP, 1, BLK),
        w_query,
        w_key,
        w_value,
        w_out,
        prompt_keys.reshape(HALF, HD),
        prompt_values.reshape(HALF, HD),
        gen_keys.reshape(OWN * GEN, HD),
        gen_values.reshape(OWN * GEN, HD),
        lengths,
        parents,
    ]
    anywhere = pl.BlockSpec(memory_space=pltpu.HBM)
    return pl.pallas_call(
        kernel,
        out_shape=jax.ShapeDtypeStruct((STEPS, OWN, BLK), bf16),
        in_specs=[anywhere] * 12,
        out_specs=pl.BlockSpec(memory_space=pltpu.VMEM),
        scratch_shapes=[
            pltpu.VMEM((GROUP, STEPS, OWN, BLK), bf16),
            pltpu.VMEM((2 * ROWS, D), bf16),
            pltpu.VMEM((TP, 1, BLK), f32),
            pltpu.VMEM((D, 2 * HD), bf16),
            pltpu.VMEM((2, D, HD), bf16),
            pltpu.VMEM((2 * HD, D), bf16),
            pltpu.VMEM((2, KEYS, HD), bf16),
            pltpu.SMEM((32,), jnp.int32),
            pltpu.SMEM((STEPS, 256), jnp.int32),
            pltpu.VMEM((2 * ROWS, KEYS), f32),
            pltpu.VMEM((2, 4 * ROWS, HD), bf16),
            pltpu.VMEM((2, 4 * ROWS, HD), f32),
            pltpu.VMEM((4 * ROWS, HD), bf16),
            pltpu.VMEM((TP, ROWS, BLK), bf16),
            pltpu.VMEM((TP, ROWS, BLK), bf16),
            pltpu.VMEM((ROWS, 2 * BLK + HD), bf16),
            pltpu.VMEM((2, TP - 2, ROWS, 2 * BLK + HD), bf16),
            pltpu.SemaphoreType.DMA((FAR_HERE + 1,)),
        ],
        compiler_params=pltpu.CompilerParams(
            collective_id=0, has_side_effects=True, vmem_limit_bytes=24 * 2**20
        ),
        name="decode_block",
    )(*[pltpu.with_memory_space_constraint(x, pltpu.HBM) for x in operands])


def solution(mesh):
    in_specs = (
        P(None, "req", "tp"),
        P(),
        P(None, "tp"),
        P(None, "tp"),
        P(None, "tp"),
        P("tp", None),
        P("req", None, "tp"),
        P("req", None, "tp"),
        P("req", None, "tp"),
        P("req", None, "tp"),
        P(),
        P(),
    )
    out_specs = P(None, "req", "tp")
    return jax.shard_map(body, mesh=mesh, in_specs=in_specs, out_specs=out_specs, check_vma=False)
```
